32 devices in a mesh: gx: 8 (over y, x, core), gy: 4 (over z).
Axes of the slice: x: 2, y: 2, z: 4, core: 2. Of those that a mesh axis runs over, the one named last changes fastest.
Arguments:
- fine_nodes: bfloat16 [32, 8, 128, 512], P('gx', 'gy'), may hold values from -6 to 6
- edge_states: bfloat16 [8, 4, 64, 128, 512], P('gx', 'gy'), may hold values from -6 to 6
- middle_nodes: bfloat16 [8, 4, 128, 512], P('gx', 'gy'), may hold values from -6 to 6
- coarse_nodes: bfloat16 [256, 512], P(('gx', 'gy')), may hold values from -6 to 6
- edge_sources: int32 [8, 4, 64, 128], P('gx', 'gy'), may hold values from 0 to 3071, as said below
- target_blocks: int32 [8, 4, 64], P('gx', 'gy'), may hold values from 0 to 7
- target_nodes: int32 [8, 4, 64, 128], P('gx', 'gy'), may hold values from 0 to 127
- live_blocks: int32 [8, 4], P('gx', 'gy'), may hold values from 32 to 64, as said below
- fine_parent: int32 [32, 8, 128], P('gx', 'gy'), may hold values from 0 to 127
- fine_weight: float32 [32, 8, 128], P('gx', 'gy'), may hold values from 0.2 to 0.6
- middle_parent: int32 [8, 4, 128], P('gx', 'gy'), may hold values from 0 to 255, as said below
- middle_weight: float32 [8, 4, 128], P('gx', 'gy'), may hold values from 0.1 to 0.3
- edge_in: bfloat16 [3, 512, 512], replicated, may hold values from -0.15625 to 0.15625
- edge_bias: float32 [512], replicated, may hold values from -3 to 3
- edge_out: bfloat16 [512, 512], replicated, may hold values from -0.25 to 0.25
- edge_bias_two: float32 [512], replicated, may hold values from -3 to 3
- edge_gain: float32 [512], replicated, may hold values from 0.1 to 1.9
- node_in: bfloat16 [2, 512, 512], replicated, may hold values from -0.1875 to 0.1875
- node_bias: float32 [512], replicated, may hold values from -3 to 3
- node_out: bfloat16 [512, 512], replicated, may hold values from -0.25 to 0.25
- node_bias_two: float32 [512], replicated, may hold values from -3 to 3
- node_gain: float32 [512], replicated, may hold values from 0.1 to 1.9
- coarse_in: bfloat16 [2, 512, 512], replicated, may hold values from -0.1875 to 0.1875
- coarse_bias: float32 [512], replicated, may hold values from -3 to 3
- coarse_out: bfloat16 [512, 512], replicated, may hold values from -0.25 to 0.25
- coarse_bias_two: float32 [512], replicated, may hold values from -3 to 3
- coarse_gain: float32 [512], replicated, may hold values from 0.1 to 1.9
Outputs:
- fine_result: bfloat16 [32, 8, 128, 512], P('gx', 'gy')
- edge_result: bfloat16 [8, 4, 64, 128, 512], P('gx', 'gy')
- middle_result: bfloat16 [8, 4, 128, 512], P('gx', 'gy')
- coarse_result: bfloat16 [256, 512], P(('gx', 'gy'))
The draws below stay inside these ranges and needn't reach their ends.
Inputs may be any that keep to these rules, and one draw needn't show every extreme that they name: `edge_sources`: sources lie in the device's own blocks or in the blocks touching them (diagonals too), never outside the grid. `live_blocks`: some device has all 64 slots live in every draw. `middle_parent`: coarse node c is owned by device c // 8 in the order of gx+gy. Of the 128 middle nodes of one device, exactly 4 have their parent among the coarse nodes of each owner.
All inputs are finite; a program needn't handle non-finite values.
Results may differ from the reference program's by a relative error of at most 0.0075.
Values may be sent and summed in bfloat16 or wider, within the bound.
A program may use at most 192 MiB of HBM per device.

```python
import jax
import jax.numpy as jnp
from jax import lax

D = 512
BLK = 128
BX = 4
BY = 2
EB = 64
CO_DEV = 8
MID_DEV = 128
NC = 256
CAP = 4
N_GX = 8
N_GY = 4


def draw_edge_sources(key, part):
    full_shape = (N_GX, N_GY, EB, BLK)
    horizontal_position = lax.broadcasted_iota(jnp.int32, full_shape, 0)
    along_y = lax.broadcasted_iota(jnp.int32, full_shape, 1)
    low_x = jnp.where(horizontal_position == 0, 1, 0)
    high_x = jnp.where(horizontal_position == N_GX - 1, BX + 1, BX + 2)
    low_y = jnp.where(along_y == 0, 1, 0)
    high_y = jnp.where(along_y == N_GY - 1, BY + 1, BY + 2)
    subkeys = jax.random.split(jax.random.fold_in(key, 11), 3)
    block_x = jax.random.randint(subkeys[0], full_shape, low_x, high_x)
    block_y = jax.random.randint(subkeys[1], full_shape, low_y, high_y)
    node_index = jax.random.randint(subkeys[2], full_shape, 0, BLK)
    return ((block_x * (BY + 2) + block_y) * BLK + node_index).astype(jnp.int32)


def draw_live_blocks(key, part):
    subkeys = jax.random.split(jax.random.fold_in(key, 23), 2)
    counts = jax.random.randint(subkeys[0], (N_GX * N_GY,), EB // 2, EB + 1)
    busiest = jax.random.randint(subkeys[1], (), 0, N_GX * N_GY)
    counts = jnp.where(jnp.arange(N_GX * N_GY) == busiest, EB, counts)
    return counts.reshape(N_GX, N_GY).astype(jnp.int32)


def draw_middle_parent(key, part):
    device_total = N_GX * N_GY
    subkeys = jax.random.split(jax.random.fold_in(key, 37), 2)
    device_keys = jax.random.split(subkeys[0], device_total)
    orders = jax.vmap(lambda one_key: jax.random.permutation(one_key, MID_DEV))(device_keys).astype(jnp.int32)
    owners = orders // CAP
    inside_block_mask = jax.random.randint(subkeys[1], (device_total, MID_DEV), 0, CO_DEV)
    return (owners * CO_DEV + inside_block_mask).reshape(N_GX, N_GY, MID_DEV).astype(jnp.int32)


def set_ends(entries, own_key, least, largest):
    longest = entries.shape.index(max(entries.shape))
    spots = []
    for shift in (0, 1):
        where = [jax.random.randint(jax.random.fold_in(own_key, axis), (), 0, length) for axis, length in enumerate(entries.shape)]
        where[longest] = (where[longest] + shift) % entries.shape[longest]
        spots.append(tuple(where))
    return entries.at[spots[0]].set(least).at[spots[1]].set(largest)


def block_levels(rng, shape, pieces, smallest, high):
    factor_of = 1.0
    for position, shards_of in pieces:
        heights = jax.random.uniform(jax.random.fold_in(jax.random.fold_in(rng, 6), position), (shards_of,), jnp.float32, smallest / len(pieces), high / len(pieces))
        factor_of = factor_of * jnp.repeat(jnp.exp(heights), shape[position] // shards_of).reshape((-1,) + (1,) * (len(shape) - 1 - position))
    return factor_of


def noise(stream_key, shape, scale, most, cuts=(), dtype=jnp.bfloat16):
    values = scale * jax.random.normal(stream_key, shape, jnp.float32)
    if cuts:
        values = values * block_levels(stream_key, shape, cuts, -0.22, 0.18)
    return jnp.clip(values, -most, most).astype(dtype)


def setup_inputs(seed: int = 0) -> dict:
    key_list = jax.random.split(jax.random.key(seed), 28)
    return {
        "fine_nodes": noise(key_list[0], (N_GX * BX, N_GY * BY, BLK, D), 1.0, 6.0, ((0, 8), (1, 4))),
        "edge_states": noise(key_list[1], (N_GX, N_GY, EB, BLK, D), 1.0, 6.0, ((0, 8), (1, 4))),
        "middle_nodes": noise(key_list[2], (N_GX, N_GY, MID_DEV, D), 1.0, 6.0, ((0, 8), (1, 4))),
        "coarse_nodes": noise(key_list[3], (NC, D), 1.0, 6.0, ((0, 32),)),
        "edge_sources": draw_edge_sources(jax.random.fold_in(key_list[27], 71), 0),
        "target_blocks": set_ends(jax.random.randint(key_list[5], (N_GX, N_GY, EB), 0, BX * BY), jax.random.fold_in(key_list[5], 1), 0, (BX * BY) - 1).astype(jnp.int32),
        "target_nodes": set_ends(jax.random.randint(key_list[6], (N_GX, N_GY, EB, BLK), 0, BLK), jax.random.fold_in(key_list[6], 1), 0, BLK - 1).astype(jnp.int32),
        "live_blocks": draw_live_blocks(jax.random.fold_in(key_list[27], 71), 0),
        "fine_parent": set_ends(jax.random.randint(key_list[8], (N_GX * BX, N_GY * BY, BLK), 0, MID_DEV), jax.random.fold_in(key_list[8], 1), 0, MID_DEV - 1).astype(jnp.int32),
        "fine_weight": jnp.clip(0.2 + 0.400000021 * jax.random.uniform(key_list[9], (N_GX * BX, N_GY * BY, BLK), jnp.float32) ** block_levels(key_list[9], (N_GX * BX, N_GY * BY, BLK), ((0, 8), (1, 4)), -0.2, 0.2), 0.2, 0.6),
        "middle_parent": draw_middle_parent(jax.random.fold_in(key_list[27], 71), 0),
        "middle_weight": jnp.clip(0.1 + 0.20000001043081284 * jax.random.uniform(key_list[11], (N_GX, N_GY, MID_DEV), jnp.float32) ** block_levels(key_list[11], (N_GX, N_GY, MID_DEV), ((0, 8), (1, 4)), -0.2, 0.2), 0.1, 0.3),
        "edge_in": noise(key_list[12], (3, D, D), (3 * D) ** -0.5, 0.15625),
        "edge_bias": noise(key_list[13], (D,), 0.5, 3.0, (), jnp.float32),
        "edge_out": noise(key_list[14], (D, D), D ** -0.5, 0.25),
        "edge_bias_two": noise(key_list[15], (D,), 0.5, 3.0, (), jnp.float32),
        "edge_gain": jnp.clip(1.0 + 0.18 * jax.random.normal(key_list[16], (D,), jnp.float32), 0.1, 1.9),
        "node_in": noise(key_list[17], (2, D, D), (2 * D) ** -0.5, 0.1875),
        "node_bias": noise(key_list[18], (D,), 0.5, 3.0, (), jnp.float32),
        "node_out": noise(key_list[19], (D, D), D ** -0.5, 0.25),
        "node_bias_two": noise(key_list[20], (D,), 0.5, 3.0, (), jnp.float32),
        "node_gain": jnp.clip(1.0 + 0.18 * jax.random.normal(key_list[21], (D,), jnp.float32), 0.1, 1.9),
        "coarse_in": noise(key_list[22], (2, D, D), (2 * D) ** -0.5, 0.1875),
        "coarse_bias": noise(key_list[23], (D,), 0.5, 3.0, (), jnp.float32),
        "coarse_out": noise(key_list[24], (D, D), D ** -0.5, 0.25),
        "coarse_bias_two": noise(key_list[25], (D,), 0.5, 3.0, (), jnp.float32),
        "coarse_gain": jnp.clip(1.0 + 0.18 * jax.random.normal(key_list[26], (D,), jnp.float32), 0.1, 1.9),
    }


epsilon = 1e-05

def layer_norm(values, gain_vec):
    centred = values - lax.optimization_barrier(jnp.mean(values, axis=-1, keepdims=True))
    spread = lax.optimization_barrier(jnp.mean(centred * centred, axis=-1, keepdims=True))
    return centred * lax.rsqrt(spread + epsilon) * gain_vec

def two_layer(pre_act, bias_one, second_weight, bias_two, gain_vec):
    hidden = jax.nn.silu(pre_act + bias_one).astype(jnp.bfloat16)
    output = jnp.dot(hidden, second_weight, preferred_element_type=jnp.float32) + bias_two
    return layer_norm(output, gain_vec)

def to_devices(array):
    tail = array.shape[3:]
    shaped = array.reshape((N_GX, BX, N_GY, BY) + array.shape[2:])
    order = (0, 2, 1, 3) + tuple(range(4, shaped.ndim))
    return shaped.transpose(order).reshape((N_GX * N_GY, BX * BY * BLK) + tail)

def from_devices(array):
    shaped = array.reshape((N_GX, N_GY, BX, BY, BLK) + array.shape[2:])
    order = (0, 2, 1, 3) + tuple(range(4, shaped.ndim))
    return shaped.transpose(order).reshape((N_GX * BX, N_GY * BY, BLK) + array.shape[2:])

def reference(fine_nodes, edge_states, middle_nodes, coarse_nodes, edge_sources, target_blocks, target_nodes, live_blocks, fine_parent, fine_weight, middle_parent, middle_weight, edge_in, edge_bias, edge_out, edge_bias_two, edge_gain, node_in, node_bias, node_out, node_bias_two, node_gain, coarse_in, coarse_bias, coarse_out, coarse_bias_two, coarse_gain):
    device_total = N_GX * N_GY
    own_count = BX * BY * BLK
    padded_all = jnp.pad(fine_nodes, ((1, 1), (1, 1), (0, 0), (0, 0)))
    parents_dev = to_devices(fine_parent)
    weights_dev = to_devices(fine_weight)
    zero_index = jnp.zeros((), jnp.int32)

    def fine_device(inputs):
        device, edge_rows, sources, block_target, node_target, live_count, parents, weights, middle_rows = inputs
        row_x = (device // N_GY).astype(jnp.int32)
        row_y = (device % N_GY).astype(jnp.int32)
        window = lax.dynamic_slice(padded_all, (row_x * BX, row_y * BY, zero_index, zero_index), (BX + 2, BY + 2, BLK, D)).reshape(-1, D)
        own_rows = lax.dynamic_slice(fine_nodes, (row_x * BX, row_y * BY, zero_index, zero_index), (BX, BY, BLK, D)).reshape(own_count, D)
        targets = (block_target[:, None] * BLK + node_target).reshape(-1).astype(jnp.int32)
        flat_edges = edge_rows.reshape(-1, D)
        from_source = jnp.take(window, sources.reshape(-1).astype(jnp.int32), axis=0)
        from_target = jnp.take(own_rows, targets, axis=0)
        pre_act = jnp.dot(flat_edges, edge_in[0], preferred_element_type=jnp.float32)
        pre_act = pre_act + jnp.dot(from_source, edge_in[1], preferred_element_type=jnp.float32)
        pre_act = pre_act + jnp.dot(from_target, edge_in[2], preferred_element_type=jnp.float32)
        message = two_layer(pre_act, edge_bias, edge_out, edge_bias_two, edge_gain).astype(jnp.bfloat16)
        active_block_mask = jnp.broadcast_to((jnp.arange(EB) < live_count)[:, None], (EB, BLK)).reshape(-1, 1)
        message = jnp.where(active_block_mask, message, jnp.zeros_like(message))
        edge_latent_updated = jnp.where(active_block_mask, (flat_edges.astype(jnp.float32) + message.astype(jnp.float32)).astype(jnp.bfloat16), flat_edges)
        aggregate = jax.ops.segment_sum(message.astype(jnp.float32), targets, num_segments=own_count).astype(jnp.bfloat16)
        node_pre = jnp.dot(own_rows, node_in[0], preferred_element_type=jnp.float32)
        node_pre = node_pre + jnp.dot(aggregate, node_in[1], preferred_element_type=jnp.float32)
        fine_mid = own_rows.astype(jnp.float32) + two_layer(node_pre, node_bias, node_out, node_bias_two, node_gain)
        restricted_mid = jax.ops.segment_sum(weights[:, None] * own_rows.astype(jnp.float32), parents.astype(jnp.int32), num_segments=MID_DEV)
        middle_mid = (middle_rows.astype(jnp.float32) + restricted_mid).astype(jnp.bfloat16)
        return (edge_latent_updated.reshape(EB, BLK, D), fine_mid, middle_mid)
    device_ids = jnp.arange(device_total).astype(jnp.int32)
    edge_latent_updated, fine_mid, middle_mid = lax.map(fine_device, (device_ids, edge_states.reshape(device_total, EB, BLK, D), edge_sources.reshape(device_total, EB, BLK), target_blocks.reshape(device_total, EB), target_nodes.reshape(device_total, EB, BLK), live_blocks.reshape(device_total), parents_dev, weights_dev, middle_nodes.reshape(device_total, MID_DEV, D)))
    mid_weights = middle_weight.reshape(device_total, MID_DEV)
    mid_parents = middle_parent.reshape(device_total, MID_DEV).astype(jnp.int32)
    weighted = (mid_weights[:, :, None] * middle_mid.astype(jnp.float32)).reshape(-1, D)
    restricted = jax.ops.segment_sum(weighted, mid_parents.reshape(-1), num_segments=NC).astype(jnp.bfloat16)
    coarse_pre = jnp.dot(coarse_nodes, coarse_in[0], preferred_element_type=jnp.float32)
    coarse_pre = coarse_pre + jnp.dot(restricted, coarse_in[1], preferred_element_type=jnp.float32)
    coarse_result = (coarse_nodes.astype(jnp.float32) + two_layer(coarse_pre, coarse_bias, coarse_out, coarse_bias_two, coarse_gain)).astype(jnp.bfloat16)
    from_coarse = jnp.take(coarse_result, mid_parents, axis=0).astype(jnp.float32)
    middle_result = (middle_mid.astype(jnp.float32) + mid_weights[:, :, None] * from_coarse).astype(jnp.bfloat16)
    from_middle = jnp.take_along_axis(middle_result, parents_dev.astype(jnp.int32)[:, :, None], axis=1).astype(jnp.float32)
    fine_flat = (fine_mid + weights_dev[:, :, None] * from_middle).astype(jnp.bfloat16)
    fine_result = from_devices(fine_flat)
    edge_result = edge_latent_updated.reshape(N_GX, N_GY, EB, BLK, D)
    return (fine_result, edge_result, middle_result.reshape(N_GX, N_GY, MID_DEV, D), coarse_result)
```

```python
import functools

import jax
import jax.numpy as jnp
from jax import lax
from jax.experimental import pallas as pl
from jax.experimental.pallas import tpu as pltpu
from jax.sharding import PartitionSpec as P

epsilon = 1e-05
f32 = jnp.float32
bf16 = jnp.bfloat16
GROUP = 4
UNITS = 8
AHEAD = 2
LANES = 128
VMEM = 64 * 1024 * 1024


def layer_norm(values, gain_vec):
    centred = values - jnp.mean(values, axis=-1, keepdims=True)
    spread = jnp.mean(centred * centred, axis=-1, keepdims=True)
    return centred * lax.rsqrt(spread + epsilon) * gain_vec


def first_dims(left, right):
    return lax.dot_general(left, right, (((0,), (0,)), ((), ())), preferred_element_type=f32)


def split_two(values):
    high = values.astype(bf16)
    return high, (values - high.astype(f32)).astype(bf16)


def activate(half):
    return half + half * jnp.tanh(half)


def centred_rows(weights):
    wide = weights.astype(f32)
    return (wide - jnp.mean(wide, axis=-1, keepdims=True)).astype(bf16)


def norm_centred(centred, gain_vec):
    spread = jnp.mean(centred * centred, axis=-1, keepdims=True)
    return centred * lax.rsqrt(spread + epsilon) * gain_vec


def exchange_kernel(
    grid_shape,
    own_hbm,
    mid_ref,
    parent_ref,
    weight_ref,
    mid_parent_ref,
    mid_weight_ref,
    coarse_ref,
    win_hbm,
    bias_ref,
    wout_hbm,
    bias_two_ref,
    gain_ref,
    edges_hbm,
    edge_in_hbm,
    tb_ref,
    tgt_ref,
    src_ref,
    window_ref,
    everyone_ref,
    result_ref,
    middle_ref,
    pre_hbm,
    index_ref,
    partial,
    arrived_x,
    summed_x,
    arrived_y,
    own_v,
    win_v,
    wout_v,
    first_w,
    target_w,
    edges_v,
    pre_v,
    target_table,
    load_sem,
    edge_load,
    pre_store,
    side_send,
    side_recv,
    edge_send,
    edge_recv,
    corner_send,
    corner_recv,
    sx_send,
    sx_recv,
    sy_send,
    sy_recv,
    gx_send,
    gx_recv,
    gy_send,
    gy_recv,
):
    count_x, count_y = grid_shape
    rows_x, rows_y, blk, width = own_hbm.shape
    mids = mid_ref.shape[0]
    chunks = edge_load.shape[0]
    chunk_rows = edges_v.shape[0] // chunks
    at_x, at_y = lax.axis_index("gx"), lax.axis_index("gy")
    peers_x = [lax.rem(at_x + offset, count_x) for offset in range(1, count_x)]
    peers_y = [lax.rem(at_y + offset, count_y) for offset in range(1, count_y)]
    mesh_ids = pl.DeviceIdType.MESH

    barrier = pltpu.get_barrier_semaphore()
    for x in peers_x:
        pl.semaphore_signal(barrier, inc=1, device_id=(x, at_y), device_id_type=mesh_ids)
    for y in peers_y:
        pl.semaphore_signal(barrier, inc=1, device_id=(at_x, y), device_id_type=mesh_ids)

    loads = [
        pltpu.make_async_copy(own_hbm, own_v, load_sem.at[0]),
        pltpu.make_async_copy(edge_in_hbm.at[2], target_w, load_sem.at[1]),
        pltpu.make_async_copy(edge_in_hbm.at[0], first_w, load_sem.at[2]),
        pltpu.make_async_copy(win_hbm, win_v, load_sem.at[3]),
        pltpu.make_async_copy(wout_hbm, wout_v, load_sem.at[4]),
    ]

    def edge_chunk(i):
        rows = pl.ds(i * chunk_rows, chunk_rows)
        return pltpu.make_async_copy(edges_hbm.at[rows], edges_v.at[rows], edge_load.at[i])

    def pre_chunk(i):
        rows = pl.ds(i * chunk_rows, chunk_rows)
        return pltpu.make_async_copy(pre_v.at[rows], pre_hbm.at[rows], pre_store.at[i])

    for load in loads:
        load.start()
    for i in range(chunks):
        edge_chunk(i).start()
    index_ref[...] = src_ref[...] * (width // LANES)
    pl.semaphore_wait(barrier, count_x + count_y - 2)

    def remote(src, dst, send, recv, x, y):
        return pltpu.make_async_remote_copy(
            src_ref=src,
            dst_ref=dst,
            send_sem=send,
            recv_sem=recv,
            device_id=(x, y),
            device_id_type=mesh_ids,
        )

    def has_x(x):
        return (x >= 0) & (x < count_x)

    def has_y(y):
        return (y >= 0) & (y < count_y)

    pieces = [(0, 1), (rows_x - 1, 1)] + ([(1, rows_x - 2)] if rows_x > 2 else [])
    ways = [1, -1]

    def side_copy(way, piece, y):
        first, length = pieces[piece]
        column = rows_y - 1 if ways[way] == 1 else 0
        to = 0 if ways[way] == 1 else rows_y + 1
        return remote(
            own_hbm.at[pl.ds(first, length), pl.ds(column, 1)],
            window_ref.at[pl.ds(first + 1, length), pl.ds(to, 1)],
            side_send.at[way, piece],
            side_recv.at[way, piece],
            at_x,
            y,
        )

    def edge_copy(way, x):
        row = rows_x - 1 if ways[way] == 1 else 0
        to = 0 if ways[way] == 1 else rows_x + 1
        return remote(
            own_hbm.at[row], window_ref.at[to, pl.ds(1, rows_y)], edge_send.at[way], edge_recv.at[way], x, at_y
        )

    def corner_copy(way, side, x):
        row = rows_x if ways[way] == 1 else 1
        to = 0 if ways[way] == 1 else rows_x + 1
        column = 0 if ways[side] == 1 else rows_y + 1
        return remote(
            window_ref.at[row, column],
            window_ref.at[to, column],
            corner_send.at[way, side],
            corner_recv.at[way, side],
            x,
            at_y,
        )

    def start_sides(piece):
        for way in range(2):

            @pl.when(has_y(at_y + ways[way]))
            def _():
                side_copy(way, piece, at_y + ways[way]).start()

    def sum_x_copy(slot_from, slot_to, x):
        return remote(
            partial.at[slot_from], arrived_x.at[slot_to], sx_send.at[slot_from], sx_recv.at[slot_to], x, at_y
        )

    def sum_y_copy(slot_from, slot_to, y):
        return remote(
            summed_x.at[slot_from], arrived_y.at[slot_to], sy_send.at[slot_from], sy_recv.at[slot_to], at_x, y
        )

    def full_y_copy(slot, y):
        here = everyone_ref.at[at_x, slot]
        return remote(here, here, gy_send.at[y], gy_recv.at[slot], at_x, y)

    def full_x_copy(slot, x):
        here = everyone_ref.at[slot]
        return remote(here, here, gx_send.at[x], gx_recv.at[slot], x, at_y)

    for piece in range(len(pieces)):
        start_sides(piece)
    for way in range(2):

        @pl.when(has_x(at_x + ways[way]))
        def _():
            edge_copy(way, at_x + ways[way]).start()

    loads[0].wait()
    own = own_v[...].reshape(rows_x * rows_y * blk, width)
    ids = lax.broadcasted_iota(jnp.int32, (mids, own.shape[0]), 0)
    high, low = split_two(jnp.where(ids == parent_ref[...], weight_ref[...], 0.0))
    middle = mid_ref[...].astype(f32) + jnp.dot(high, own, preferred_element_type=f32)
    middle = (middle + jnp.dot(low, own, preferred_element_type=f32)).astype(bf16)
    ids = lax.broadcasted_iota(jnp.int32, (count_x * count_y * coarse_ref.shape[0], mids), 0)
    high, low = split_two(jnp.where(ids == mid_parent_ref[...], mid_weight_ref[...], 0.0))
    sums = jnp.dot(high, middle, preferred_element_type=f32)
    sums = sums + jnp.dot(low, middle, preferred_element_type=f32)
    partial[...] = sums.reshape(partial.shape)
    middle_ref[...] = middle

    for x in peers_x:
        sum_x_copy(x, at_x, x).start()

    loads[1].wait()
    for a in range(rows_x):
        for b in range(rows_y):
            made = jnp.dot(own_v[a, b], target_w[...], preferred_element_type=f32) * 0.5
            target_table[a * rows_y + b] = made.astype(bf16)
    loads[2].wait()
    first_w[...] = first_w[...] * 0.5

    rows = GROUP * blk

    def group(g, carry):
        at = pl.ds(pl.multiple_of(g * rows, rows), rows)
        from_target = []
        for k in range(GROUP):
            number = g * GROUP + k
            target = tgt_ref[pl.ds(number, 1), :]
            pick = (lax.broadcasted_iota(jnp.int32, (blk, blk), 0) == target).astype(f32).astype(bf16)
            from_target.append(first_dims(pick, target_table[tb_ref[number]]))
        made = jnp.dot(edges_v[at, :], first_w[...], preferred_element_type=f32)
        pre_v[at, :] = (made + jnp.concatenate(from_target, axis=0)).astype(bf16)
        return carry

    def work(first, last):
        for i in range(first, last):
            edge_chunk(i).wait()
        lax.fori_loop(first * (chunk_rows // rows), last * (chunk_rows // rows), group, 0)
        for i in range(first, last):
            pre_chunk(i).start()

    marks = [(chunks * part) // 8 for part in range(9)]

    work(marks[0], marks[3])

    total = partial[at_x]
    for x in peers_x:
        sum_x_copy(x, x, x).wait_recv()
        total = total + arrived_x[x]
    summed_x[...] = total
    for y in peers_y:
        sum_y_copy(y, at_y, y).start()

    work(marks[3], marks[5])

    for side in range(2):
        from_y = at_y - ways[side]

        @pl.when(has_y(from_y))
        def _():
            side_copy(side, 0, from_y).wait_recv()
            side_copy(side, 1, from_y).wait_recv()
            for way in range(2):

                @pl.when(has_x(at_x + ways[way]))
                def _():
                    corner_copy(way, side, at_x + ways[way]).start()

    restricted = summed_x[at_y]
    for y in peers_y:
        sum_y_copy(y, y, y).wait_recv()
        restricted = restricted + arrived_y[y]

    loads[3].wait()
    loads[4].wait()
    coarse = coarse_ref[...]
    pre = jnp.dot(coarse, win_v[0], preferred_element_type=f32)
    pre = pre + jnp.dot(restricted.astype(bf16), win_v[1], preferred_element_type=f32)
    hidden = activate((pre + bias_ref[...]) * 0.5).astype(bf16)
    output = jnp.dot(hidden, wout_v[...], preferred_element_type=f32) + bias_two_ref[...]
    result = (coarse.astype(f32) + layer_norm(output, gain_ref[...])).astype(bf16)
    everyone_ref[at_x, at_y] = result
    result_ref[...] = result
    for y in peers_y:
        full_y_copy(at_y, y).start()

    work(marks[5], marks[7])

    for y in peers_y:
        full_y_copy(y, y).wait_recv()
    for x in peers_x:
        full_x_copy(at_x, x).start()

    work(marks[7], marks[8])

    for way in range(2):

        @pl.when(has_x(at_x - ways[way]))
        def _():
            edge_copy(way, at_x - ways[way]).wait_recv()

        @pl.when(has_x(at_x + ways[way]))
        def _():
            edge_copy(way, at_x + ways[way]).wait_send()

        @pl.when(has_y(at_y + ways[way]))
        def _():
            for piece in range(len(pieces)):
                side_copy(way, piece, at_y + ways[way]).wait_send()

        if len(pieces) > 2:

            @pl.when(has_y(at_y - ways[way]))
            def _():
                side_copy(way, 2, at_y - ways[way]).wait_recv()

        for side in range(2):

            @pl.when(has_y(at_y - ways[side]) & has_x(at_x + ways[way]))
            def _():
                corner_copy(way, side, at_x + ways[way]).wait_send()

            @pl.when(has_y(at_y - ways[side]) & has_x(at_x - ways[way]))
            def _():
                corner_copy(way, side, at_x - ways[way]).wait_recv()

    for x in peers_x:
        sum_x_copy(x, at_x, x).wait_send()
        full_x_copy(at_x, x).wait_send()
        full_x_copy(x, x).wait_recv()
    for y in peers_y:
        sum_y_copy(y, at_y, y).wait_send()
        full_y_copy(at_y, y).wait_send()
    for i in range(chunks):
        pre_chunk(i).wait()


def exchange(own, middle, parents, weights, mid_parents, mid_weights, coarse, params, edges, edge_in, tb, tgt, src):
    rows_x, rows_y, blk, width = own.shape
    count_x, count_y = lax.axis_size("gx"), lax.axis_size("gy")
    coarse_own = coarse.shape[0]
    coarse_in, bias, coarse_out, bias_two, gain = params
    row = lambda array: array.reshape(1, -1)
    vmem = pl.BlockSpec(memory_space=pltpu.VMEM)
    smem = pl.BlockSpec(memory_space=pltpu.SMEM)
    hbm = pl.BlockSpec(memory_space=pl.ANY)
    dma = pltpu.SemaphoreType.DMA
    chunks = src.shape[0] // UNITS
    return pl.pallas_call(
        functools.partial(exchange_kernel, (count_x, count_y)),
        in_specs=[hbm] + [vmem] * 6 + [hbm, vmem, hbm, vmem, vmem, hbm, hbm, smem, vmem, vmem],
        out_specs=[hbm, vmem, vmem, vmem, hbm, vmem],
        out_shape=[
            jax.ShapeDtypeStruct((rows_x + 2, rows_y + 2, blk, width), bf16),
            jax.ShapeDtypeStruct((count_x, count_y, coarse_own, width), bf16),
            jax.ShapeDtypeStruct((coarse_own, width), bf16),
            jax.ShapeDtypeStruct(middle.shape, bf16),
            jax.ShapeDtypeStruct(edges.shape, bf16),
            jax.ShapeDtypeStruct(src.shape, jnp.int32),
        ],
        scratch_shapes=[
            pltpu.VMEM((count_x, count_y, coarse_own, width), f32),
            pltpu.VMEM((count_x, count_y, coarse_own, width), f32),
            pltpu.VMEM((count_y, coarse_own, width), f32),
            pltpu.VMEM((count_y, coarse_own, width), f32),
            pltpu.VMEM(own.shape, bf16),
            pltpu.VMEM(coarse_in.shape, bf16),
            pltpu.VMEM(coarse_out.shape, bf16),
            pltpu.VMEM(edge_in.shape[1:], bf16),
            pltpu.VMEM(edge_in.shape[1:], bf16),
            pltpu.VMEM(edges.shape, bf16),
            pltpu.VMEM(edges.shape, bf16),
            pltpu.VMEM((rows_x * rows_y, blk, width), bf16),
            dma((5,)),
            dma((chunks,)),
            dma((chunks,)),
            dma((2, 3)),
            dma((2, 3)),
            dma((2,)),
            dma((2,)),
            dma((2, 2)),
            dma((2, 2)),
            dma((count_x,)),
            dma((count_x,)),
            dma((count_y,)),
            dma((count_y,)),
            dma((count_x,)),
            dma((count_x,)),
            dma((count_y,)),
            dma((count_y,)),
        ],
        compiler_params=pltpu.CompilerParams(
            collective_id=0, has_side_effects=True, vmem_limit_bytes=VMEM
        ),
        name="exchange",
    )(
        own,
        middle,
        row(parents),
        row(weights),
        row(mid_parents),
        row(mid_weights),
        coarse,
        coarse_in,
        row(bias),
        coarse_out,
        row(bias_two),
        row(gain),
        edges,
        edge_in,
        tb,
        tgt,
        src,
    )


def edge_kernel(
    shape,
    index_ref,
    tb_ref,
    live_ref,
    pre_ref,
    edge_ref,
    tgt_ref,
    bias_ref,
    bias_two_ref,
    gain_ref,
    parent_ref,
    weight_ref,
    mid_ref,
    mid_parent_ref,
    mid_weight_ref,
    coarse_ref,
    coarse_own_ref,
    node_bias_ref,
    node_bias_two_ref,
    node_gain_ref,
    own_hbm,
    window_hbm,
    edge_in_hbm,
    wout_hbm,
    node_in_hbm,
    node_out_hbm,
    out_ref,
    fine_ref,
    mid_out_ref,
    coarse_out_ref,
    table,
    bufs,
    made_out,
    total,
    own_v,
    window_v,
    source_w,
    wout_v,
    node_in_v,
    node_out_v,
    bias_two_c,
    node_bias_two_c,
    doubled,
    load_sem,
):
    rows_x, rows_y, blk, width = shape
    parts = width // LANES
    step = pl.program_id(0)
    steps = pl.num_programs(0)
    live = live_ref[0]
    mids = mid_ref.shape[0]
    copy = pltpu.make_async_copy

    loads = [
        copy(edge_in_hbm.at[1], source_w, load_sem.at[0]),
        copy(own_hbm, own_v, load_sem.at[1]),
        copy(window_hbm, window_v, load_sem.at[2]),
        copy(wout_hbm, wout_v, load_sem.at[3]),
        copy(node_in_hbm, node_in_v, load_sem.at[4]),
        copy(node_out_hbm, node_out_v, load_sem.at[5]),
    ]

    def gather(number, slot):
        view = index_ref.at[pl.ds(pl.multiple_of(number * blk, blk), blk)]
        for e in range(blk):
            at = (e // 8) * (8 * parts) + e % 8
            row = pl.multiple_of(view[e], parts)
            bufs[slot, pl.ds(at, parts, stride=8), :] = table[pl.ds(row, parts), :]

    def second(u):
        found = bufs[u % 4].reshape(blk // 8, parts, 8, LANES)
        found = jnp.concatenate([found[:, c].reshape(blk, LANES) for c in range(parts)], axis=1)
        half = pre_ref[pl.ds(u * blk, blk), :].astype(f32) + found
        hidden = activate(half).astype(bf16)
        made_out[u % 2] = jnp.dot(hidden, wout_v[...], preferred_element_type=f32) + bias_two_c[...]

    def finish(u):
        number = step * UNITS + u
        centred = made_out[u % 2]
        alive = (number < live).astype(f32)
        spread = jnp.mean(centred * centred, axis=-1, keepdims=True)
        message = (centred * (lax.rsqrt(spread + epsilon) * alive) * gain_ref[...]).astype(bf16)
        at = pl.ds(u * blk, blk)
        out_ref[at, :] = edge_ref[at, :] + message
        target = tgt_ref[pl.ds(u, 1), :]
        pick = (lax.broadcasted_iota(jnp.int32, (blk, blk), 0) == target).astype(f32).astype(bf16)
        here = pl.multiple_of(tb_ref[number] * blk, blk)
        total[pl.ds(here, blk), :] += jnp.dot(pick, message, preferred_element_type=f32)

    @pl.when(step == 0)
    def _():
        for load in loads:
            load.start()
        total[...] = jnp.zeros_like(total)
        coarse_out_ref[...] = coarse_own_ref[...]
        bias_two = bias_two_ref[...]
        bias_two_c[...] = bias_two - jnp.mean(bias_two, axis=-1, keepdims=True)
        bias_two = node_bias_two_ref[...]
        node_bias_two_c[...] = bias_two - jnp.mean(bias_two, axis=-1, keepdims=True)
        loads[0].wait()
        loads[1].wait()

        def fill(number, rows):
            made = jnp.dot(rows, source_w[...], preferred_element_type=f32)
            made = (made + bias_ref[...]) * 0.5
            for c in range(parts):
                at = pl.ds(number * blk * parts + c, blk, stride=parts)
                table[at, :] = made[:, c * LANES : (c + 1) * LANES]

        inner = [(a, b) for a in range(1, rows_x + 1) for b in range(1, rows_y + 1)]
        outer = [(a, b) for a in range(rows_x + 2) for b in range(rows_y + 2) if (a, b) not in inner]
        for a, b in inner:
            fill(a * (rows_y + 2) + b, own_v[a - 1, b - 1])
        loads[2].wait()
        for a, b in outer:
            fill(a * (rows_y + 2) + b, window_v[a, b])
        loads[3].wait()
        wout_v[...] = centred_rows(wout_v[...])
        for u in range(AHEAD):
            gather(u, u % 4)

    @pl.when(step * UNITS < live)
    def _():
        second(0)
        for u in range(UNITS):
            following = jnp.minimum(step * UNITS + u + AHEAD, steps * UNITS - 1)
            gather(following, (u + AHEAD) % 4)
            if u + 1 < UNITS:
                second(u + 1)
            finish(u)

    @pl.when(step * UNITS >= live)
    def _():
        out_ref[...] = edge_ref[...]

    @pl.when(step == steps - 1)
    def _():
        coarse = coarse_ref[...]
        ids = lax.broadcasted_iota(jnp.int32, (coarse.shape[0], mids), 0)
        high, low = split_two(jnp.where(ids == mid_parent_ref[...], mid_weight_ref[...], 0.0))
        value = mid_ref[...].astype(f32) + first_dims(high, coarse) + first_dims(low, coarse)
        value = value.astype(bf16)
        mid_out_ref[...] = value
        doubled[pl.ds(0, mids), :] = value
        doubled[pl.ds(mids, mids), :] = value
        loads[4].wait()
        loads[5].wait()
        node_out_v[...] = centred_rows(node_out_v[...])
        for a in range(rows_x):
            for b in range(rows_y):
                at = pl.ds((a * rows_y + b) * blk, blk)
                own = own_v[a, b]
                pre = jnp.dot(own, node_in_v[0], preferred_element_type=f32)
                pre = pre + jnp.dot(total[at, :].astype(bf16), node_in_v[1], preferred_element_type=f32)
                hidden = activate((pre + node_bias_ref[...]) * 0.5).astype(bf16)
                centred = jnp.dot(hidden, node_out_v[...], preferred_element_type=f32) + node_bias_two_c[...]
                fine = own.astype(f32) + norm_centred(centred, node_gain_ref[...])
                ids = lax.broadcasted_iota(jnp.int32, (mids, blk), 0)
                high, low = split_two(jnp.where(ids == parent_ref[:, at], weight_ref[:, at], 0.0))
                from_middle = first_dims(jnp.concatenate([high, low], axis=0), doubled[...])
                fine_ref[at, :] = (fine + from_middle).astype(bf16)


def run_edges(own, window, pre, edges, index, block_target, node_target, live, edge_params, nodes, node_params):
    rows_x, rows_y, blk, width = own.shape
    edge_in, bias, edge_out, bias_two, gain = edge_params
    node_in, node_bias, node_out, node_bias_two, node_gain = node_params
    parents, weights, middle, mid_parents, mid_weights, coarse, coarse_own = nodes
    edge_blocks = index.shape[0]
    whole = lambda array: pl.BlockSpec(array.shape, lambda i, *_: (0,) * array.ndim)
    row = lambda array: array.reshape(1, -1)
    targets = node_target.reshape(edge_blocks // UNITS, UNITS, blk)
    own_count = rows_x * rows_y * blk
    row_spec = pl.BlockSpec((UNITS * blk, width), lambda i, *_: (i, 0))
    hbm = pl.BlockSpec(memory_space=pl.ANY)
    small = [row(bias), row(bias_two), row(gain), row(parents), row(weights), middle]
    small += [row(mid_parents), row(mid_weights), coarse, coarse_own]
    small += [row(node_bias), row(node_bias_two), row(node_gain)]
    large = [own, window, edge_in, edge_out, node_in, node_out]
    fine = jax.ShapeDtypeStruct((own_count, width), bf16)
    return pl.pallas_call(
        functools.partial(edge_kernel, own.shape),
        grid_spec=pltpu.PrefetchScalarGridSpec(
            num_scalar_prefetch=3,
            grid=(edge_blocks // UNITS,),
            in_specs=[row_spec, row_spec, pl.BlockSpec((None, UNITS, blk), lambda i, *_: (i, 0, 0))]
            + [whole(s) for s in small]
            + [hbm] * len(large),
            out_specs=[row_spec, whole(fine), whole(middle), whole(coarse_own)],
            scratch_shapes=[
                pltpu.VMEM(((rows_x + 2) * (rows_y + 2) * blk * (width // LANES), LANES), f32),
                pltpu.VMEM((4, blk * width // LANES, LANES), f32),
                pltpu.VMEM((2, blk, width), f32),
                pltpu.VMEM((own_count, width), f32),
                pltpu.VMEM(own.shape, bf16),
                pltpu.VMEM(window.shape, bf16),
                pltpu.VMEM(edge_in.shape[1:], bf16),
                pltpu.VMEM(edge_out.shape, bf16),
                pltpu.VMEM(node_in.shape, bf16),
                pltpu.VMEM(node_out.shape, bf16),
                pltpu.VMEM((1, width), f32),
                pltpu.VMEM((1, width), f32),
                pltpu.VMEM((2 * middle.shape[0], width), bf16),
                pltpu.SemaphoreType.DMA((6,)),
            ],
        ),
        out_shape=[
            jax.ShapeDtypeStruct(edges.shape, bf16),
            fine,
            jax.ShapeDtypeStruct(middle.shape, bf16),
            jax.ShapeDtypeStruct(coarse_own.shape, bf16),
        ],
        compiler_params=pltpu.CompilerParams(vmem_limit_bytes=VMEM),
        name="edge_node_layer",
    )(index.reshape(-1), block_target, live.reshape(1), pre, edges, targets, *small, *large)


def body(
    fine_nodes,
    edge_states,
    middle_nodes,
    coarse_nodes,
    edge_sources,
    target_blocks,
    target_nodes,
    live_blocks,
    fine_parent,
    fine_weight,
    middle_parent,
    middle_weight,
    edge_in,
    edge_bias,
    edge_out,
    edge_bias_two,
    edge_gain,
    node_in,
    node_bias,
    node_out,
    node_bias_two,
    node_gain,
    coarse_in,
    coarse_bias,
    coarse_out,
    coarse_bias_two,
    coarse_gain,
):
    rows_x, rows_y, block_size, latent = fine_nodes.shape
    own_count = rows_x * rows_y * block_size
    edge_params = (edge_in, edge_bias, edge_out, edge_bias_two, edge_gain)
    node_params = (node_in, node_bias, node_out, node_bias_two, node_gain)
    parents_local = fine_parent.reshape(own_count)
    weights_local = fine_weight.reshape(own_count)
    middle_rows = middle_nodes[0, 0]
    mid_parents = middle_parent[0, 0]
    mid_weights = middle_weight[0, 0]
    coarse_own = coarse_nodes.shape[0]
    devices = lax.axis_size(("gx", "gy"))
    edges = edge_states.reshape(-1, latent)
    window, everyone, coarse_own_rows, middle_mid, pre, index = exchange(
        fine_nodes,
        middle_rows,
        parents_local,
        weights_local,
        mid_parents,
        mid_weights,
        coarse_nodes,
        (coarse_in, coarse_bias, coarse_out, coarse_bias_two, coarse_gain),
        edges,
        edge_in,
        target_blocks[0, 0],
        target_nodes[0, 0],
        edge_sources[0, 0],
    )
    everyone = everyone.reshape(devices * coarse_own, latent)
    nodes = (parents_local, weights_local, middle_mid, mid_parents, mid_weights, everyone, coarse_own_rows)
    edge_result, fine_result, middle_result, coarse_result = run_edges(
        fine_nodes,
        window,
        pre,
        edges,
        index,
        target_blocks[0, 0],
        target_nodes[0, 0],
        live_blocks[0, 0],
        edge_params,
        nodes,
        node_params,
    )
    return (
        fine_result.reshape(fine_nodes.shape),
        edge_result.reshape(edge_states.shape),
        middle_result.reshape(middle_nodes.shape),
        coarse_result,
    )


def solution(mesh):
    placed = (
        P("gx", "gy", None, None),
        P("gx", "gy", None, None, None),
        P("gx", "gy", None, None),
        P(("gx", "gy"), None),
        P("gx", "gy", None, None),
        P("gx", "gy", None),
        P("gx", "gy", None, None),
        P("gx", "gy"),
        P("gx", "gy", None),
        P("gx", "gy", None),
        P("gx", "gy", None),
        P("gx", "gy", None),
        P(),
        P(),
        P(),
        P(),
        P(),
        P(),
        P(),
        P(),
        P(),
        P(),
        P(),
        P(),
        P(),
        P(),
        P(),
    )
    return jax.shard_map(
        body,
        mesh=mesh,
        in_specs=placed,
        out_specs=(
            P("gx", "gy", None, None),
            P("gx", "gy", None, None, None),
            P("gx", "gy", None, None),
            P(("gx", "gy"), None),
        ),
        check_vma=False,
    )
```

```python
import functools

import jax
import jax.numpy as jnp
from jax import lax
from jax.experimental import pallas as pl
from jax.experimental.pallas import tpu as pltpu
from jax.sharding import PartitionSpec as P

epsilon = 1e-05
f32 = jnp.float32
bf16 = jnp.bfloat16
GROUP = 4
UNITS = 8
PAIR = 2
AHEAD = 2
SLOTS = 4
LANES = 128
VMEM = 64 * 1024 * 1024


def layer_norm(values, gain_vec):
    centred = values - jnp.mean(values, axis=-1, keepdims=True)
    spread = jnp.mean(centred * centred, axis=-1, keepdims=True)
    return centred * lax.rsqrt(spread + epsilon) * gain_vec


def first_dims(left, right):
    return lax.dot_general(left, right, (((0,), (0,)), ((), ())), preferred_element_type=f32)


def split_two(values):
    high = values.astype(bf16)
    return high, (values - high.astype(f32)).astype(bf16)


def activate(half):
    return half + half * jnp.tanh(half)


def centred_rows(weights):
    wide = weights.astype(f32)
    return (wide - jnp.mean(wide, axis=-1, keepdims=True)).astype(bf16)


def norm_centred(centred, gain_vec):
    spread = jnp.mean(centred * centred, axis=-1, keepdims=True)
    return centred * lax.rsqrt(spread + epsilon) * gain_vec


def exchange_kernel(
    grid_shape,
    own_hbm,
    mid_ref,
    parent_ref,
    weight_ref,
    mid_parent_ref,
    mid_weight_ref,
    coarse_ref,
    win_hbm,
    bias_ref,
    wout_hbm,
    bias_two_ref,
    gain_ref,
    edges_hbm,
    edge_in_hbm,
    tb_ref,
    tgt_ref,
    src_ref,
    rows_ref,
    prev_ref,
    window_ref,
    everyone_ref,
    result_ref,
    middle_ref,
    pre_hbm,
    index_ref,
    partial,
    arrived_x,
    summed_x,
    arrived_y,
    own_v,
    win_v,
    wout_v,
    first_w,
    target_w,
    edges_v,
    pre_v,
    target_table,
    table,
    bufs,
    hist,
    load_sem,
    edge_load,
    pre_store,
    side_send,
    side_recv,
    edge_send,
    edge_recv,
    corner_send,
    corner_recv,
    sx_send,
    sx_recv,
    sy_send,
    sy_recv,
    gx_send,
    gx_recv,
    gy_send,
    gy_recv,
):
    count_x, count_y = grid_shape
    rows_x, rows_y, blk, width = own_hbm.shape
    mids = mid_ref.shape[0]
    chunks = edge_load.shape[0]
    chunk_rows = edges_v.shape[0] // chunks
    at_x, at_y = lax.axis_index("gx"), lax.axis_index("gy")
    peers_x = [lax.rem(at_x + offset, count_x) for offset in range(1, count_x)]
    peers_y = [lax.rem(at_y + offset, count_y) for offset in range(1, count_y)]
    mesh_ids = pl.DeviceIdType.MESH

    barrier = pltpu.get_barrier_semaphore()
    for x in peers_x:
        pl.semaphore_signal(barrier, inc=1, device_id=(x, at_y), device_id_type=mesh_ids)
    for y in peers_y:
        pl.semaphore_signal(barrier, inc=1, device_id=(at_x, y), device_id_type=mesh_ids)

    loads = [
        pltpu.make_async_copy(own_hbm, own_v, load_sem.at[0]),
        pltpu.make_async_copy(edge_in_hbm.at[2], target_w, load_sem.at[1]),
        pltpu.make_async_copy(edge_in_hbm.at[0], first_w, load_sem.at[2]),
        pltpu.make_async_copy(win_hbm, win_v, load_sem.at[3]),
        pltpu.make_async_copy(wout_hbm, wout_v, load_sem.at[4]),
    ]

    def edge_chunk(i):
        rows = pl.ds(i * chunk_rows, chunk_rows)
        return pltpu.make_async_copy(edges_hbm.at[rows], edges_v.at[rows], edge_load.at[i])

    def pre_chunk(i):
        rows = pl.ds(i * chunk_rows, chunk_rows)
        return pltpu.make_async_copy(pre_v.at[rows], pre_hbm.at[rows], pre_store.at[i])

    for load in loads[:3]:
        load.start()
    blocks = src_ref.shape[0]
    index_ref[pl.ds(0, blocks), :] = src_ref[...] * (width // LANES)
    extra = index_ref.shape[0] - blocks
    index_ref[pl.ds(blocks, extra), :] = jnp.zeros((extra, blk), jnp.int32)
    pl.semaphore_wait(barrier, count_x + count_y - 2)

    def remote(src, dst, send, recv, x, y):
        return pltpu.make_async_remote_copy(
            src_ref=src,
            dst_ref=dst,
            send_sem=send,
            recv_sem=recv,
            device_id=(x, y),
            device_id_type=mesh_ids,
        )

    def has_x(x):
        return (x >= 0) & (x < count_x)

    def has_y(y):
        return (y >= 0) & (y < count_y)

    pieces = [(0, 1), (rows_x - 1, 1)] + ([(1, rows_x - 2)] if rows_x > 2 else [])
    ways = [1, -1]

    def side_copy(way, piece, y):
        first, length = pieces[piece]
        column = rows_y - 1 if ways[way] == 1 else 0
        to = 0 if ways[way] == 1 else rows_y + 1
        return remote(
            own_hbm.at[pl.ds(first, length), pl.ds(column, 1)],
            window_ref.at[pl.ds(first + 1, length), pl.ds(to, 1)],
            side_send.at[way, piece],
            side_recv.at[way, piece],
            at_x,
            y,
        )

    def edge_copy(way, x):
        row = rows_x - 1 if ways[way] == 1 else 0
        to = 0 if ways[way] == 1 else rows_x + 1
        return remote(
            own_hbm.at[row], window_ref.at[to, pl.ds(1, rows_y)], edge_send.at[way], edge_recv.at[way], x, at_y
        )

    def corner_copy(way, side, x):
        row = rows_x if ways[way] == 1 else 1
        to = 0 if ways[way] == 1 else rows_x + 1
        column = 0 if ways[side] == 1 else rows_y + 1
        return remote(
            window_ref.at[row, column],
            window_ref.at[to, column],
            corner_send.at[way, side],
            corner_recv.at[way, side],
            x,
            at_y,
        )

    def start_sides(piece):
        for way in range(2):

            @pl.when(has_y(at_y + ways[way]))
            def _():
                side_copy(way, piece, at_y + ways[way]).start()

    def sum_x_copy(slot_from, slot_to, x):
        return remote(
            partial.at[slot_from], arrived_x.at[slot_to], sx_send.at[slot_from], sx_recv.at[slot_to], x, at_y
        )

    def sum_y_copy(slot_from, slot_to, y):
        return remote(
            summed_x.at[slot_from], arrived_y.at[slot_to], sy_send.at[slot_from], sy_recv.at[slot_to], at_x, y
        )

    def full_y_copy(slot, y):
        here = everyone_ref.at[at_x, slot]
        return remote(here, here, gy_send.at[y], gy_recv.at[slot], at_x, y)

    def full_x_copy(slot, x):
        here = everyone_ref.at[slot]
        return remote(here, here, gx_send.at[x], gx_recv.at[slot], x, at_y)

    for piece in range(len(pieces)):
        start_sides(piece)
    for way in range(2):

        @pl.when(has_x(at_x + ways[way]))
        def _():
            edge_copy(way, at_x + ways[way]).start()

    loads[0].wait()
    for i in range(chunks):
        edge_chunk(i).start()
    for load in loads[3:]:
        load.start()
    own = own_v[...].reshape(rows_x * rows_y * blk, width)
    ids = lax.broadcasted_iota(jnp.int32, (mids, own.shape[0]), 0)
    high, low = split_two(jnp.where(ids == parent_ref[...], weight_ref[...], 0.0))
    middle = mid_ref[...].astype(f32) + jnp.dot(high, own, preferred_element_type=f32)
    middle = (middle + jnp.dot(low, own, preferred_element_type=f32)).astype(bf16)
    ids = lax.broadcasted_iota(jnp.int32, (count_x * count_y * coarse_ref.shape[0], mids), 0)
    high, low = split_two(jnp.where(ids == mid_parent_ref[...], mid_weight_ref[...], 0.0))
    sums = jnp.dot(high, middle, preferred_element_type=f32)
    sums = sums + jnp.dot(low, middle, preferred_element_type=f32)
    partial[...] = sums.reshape(partial.shape)
    middle_ref[...] = middle

    for x in peers_x:
        sum_x_copy(x, at_x, x).start()

    loads[1].wait()
    made = jnp.dot(own, target_w[...], preferred_element_type=f32) * 0.5
    target_table[...] = made.astype(bf16).reshape(target_table.shape)
    loads[2].wait()
    first_w[...] = first_w[...] * 0.5

    rows = GROUP * blk

    def group(g, carry):
        at = pl.ds(pl.multiple_of(g * rows, rows), rows)
        from_target = []
        for k in range(GROUP):
            number = g * GROUP + k
            target = tgt_ref[pl.ds(number, 1), :]
            pick = (lax.broadcasted_iota(jnp.int32, (blk, blk), 0) == target).astype(f32).astype(bf16)
            from_target.append(first_dims(pick, target_table[tb_ref[number]]))
        made = jnp.dot(edges_v[at, :], first_w[...], preferred_element_type=f32)
        pre_v[at, :] = (made + jnp.concatenate(from_target, axis=0)).astype(bf16)
        return carry

    def work(first, last):
        for i in range(first, last):
            edge_chunk(i).wait()
        lax.fori_loop(first * (chunk_rows // rows), last * (chunk_rows // rows), group, 0)
        for i in range(first, last):
            pre_chunk(i).start()

    marks = [(chunks * part) // 8 for part in range(9)]

    work(marks[0], marks[3])

    total = partial[at_x]
    for x in peers_x:
        sum_x_copy(x, x, x).wait_recv()
        total = total + arrived_x[x]
    summed_x[...] = total
    for y in peers_y:
        sum_y_copy(y, at_y, y).start()

    work(marks[3], marks[5])

    for side in range(2):
        from_y = at_y - ways[side]

        @pl.when(has_y(from_y))
        def _():
            side_copy(side, 0, from_y).wait_recv()
            side_copy(side, 1, from_y).wait_recv()
            for way in range(2):

                @pl.when(has_x(at_x + ways[way]))
                def _():
                    corner_copy(way, side, at_x + ways[way]).start()

    restricted = summed_x[at_y]
    for y in peers_y:
        sum_y_copy(y, y, y).wait_recv()
        restricted = restricted + arrived_y[y]

    loads[3].wait()
    loads[4].wait()
    coarse = coarse_ref[...]
    pre = jnp.dot(coarse, win_v[0], preferred_element_type=f32)
    pre = pre + jnp.dot(restricted.astype(bf16), win_v[1], preferred_element_type=f32)
    hidden = activate((pre + bias_ref[...]) * 0.5).astype(bf16)
    output = jnp.dot(hidden, wout_v[...], preferred_element_type=f32) + bias_two_ref[...]
    result = (coarse.astype(f32) + layer_norm(output, gain_ref[...])).astype(bf16)
    everyone_ref[at_x, at_y] = result
    result_ref[...] = result
    for y in peers_y:
        full_y_copy(at_y, y).start()

    work(marks[5], marks[7])

    for y in peers_y:
        full_y_copy(y, y).wait_recv()
    for x in peers_x:
        full_x_copy(at_x, x).start()

    work(marks[7], marks[8])

    table[...] = jnp.zeros_like(table)

    def gathers(g, carry):
        for e in range(256):
            bufs[g % 2, e // 8, :, e % 8, :] = table[rows_ref[g * 256 + e]]
        hist[g + 1] = hist[prev_ref[g]] + 1.0
        return carry

    lax.fori_loop(0, chunks * 4, gathers, 0)

    for way in range(2):

        @pl.when(has_x(at_x - ways[way]))
        def _():
            edge_copy(way, at_x - ways[way]).wait_recv()

        @pl.when(has_x(at_x + ways[way]))
        def _():
            edge_copy(way, at_x + ways[way]).wait_send()

        @pl.when(has_y(at_y + ways[way]))
        def _():
            for piece in range(len(pieces)):
                side_copy(way, piece, at_y + ways[way]).wait_send()

        if len(pieces) > 2:

            @pl.when(has_y(at_y - ways[way]))
            def _():
                side_copy(way, 2, at_y - ways[way]).wait_recv()

        for side in range(2):

            @pl.when(has_y(at_y - ways[side]) & has_x(at_x + ways[way]))
            def _():
                corner_copy(way, side, at_x + ways[way]).wait_send()

            @pl.when(has_y(at_y - ways[side]) & has_x(at_x - ways[way]))
            def _():
                corner_copy(way, side, at_x - ways[way]).wait_recv()

    for x in peers_x:
        sum_x_copy(x, at_x, x).wait_send()
        full_x_copy(at_x, x).wait_send()
        full_x_copy(x, x).wait_recv()
    for y in peers_y:
        sum_y_copy(y, at_y, y).wait_send()
        full_y_copy(at_y, y).wait_send()
    for i in range(chunks):
        pre_chunk(i).wait()


def exchange(own, middle, parents, weights, mid_parents, mid_weights, coarse, params, edges, edge_in, tb, tgt, src):
    rows_x, rows_y, blk, width = own.shape
    count_x, count_y = lax.axis_size("gx"), lax.axis_size("gy")
    coarse_own = coarse.shape[0]
    coarse_in, bias, coarse_out, bias_two, gain = params
    row = lambda array: array.reshape(1, -1)
    vmem = pl.BlockSpec(memory_space=pltpu.VMEM)
    smem = pl.BlockSpec(memory_space=pltpu.SMEM)
    hbm = pl.BlockSpec(memory_space=pl.ANY)
    dma = pltpu.SemaphoreType.DMA
    chunks = src.shape[0] // UNITS
    return pl.pallas_call(
        functools.partial(exchange_kernel, (count_x, count_y)),
        in_specs=[hbm] + [vmem] * 6 + [hbm, vmem, hbm, vmem, vmem, hbm, hbm, smem, vmem, vmem, smem, smem],
        out_specs=[hbm, vmem, vmem, vmem, hbm, vmem],
        out_shape=[
            jax.ShapeDtypeStruct((rows_x + 2, rows_y + 2, blk, width), bf16),
            jax.ShapeDtypeStruct((count_x, count_y, coarse_own, width), bf16),
            jax.ShapeDtypeStruct((coarse_own, width), bf16),
            jax.ShapeDtypeStruct(middle.shape, bf16),
            jax.ShapeDtypeStruct(edges.shape, bf16),
            jax.ShapeDtypeStruct((src.shape[0] + UNITS, blk), jnp.int32),
        ],
        scratch_shapes=[
            pltpu.VMEM((count_x, count_y, coarse_own, width), f32),
            pltpu.VMEM((count_x, count_y, coarse_own, width), f32),
            pltpu.VMEM((count_y, coarse_own, width), f32),
            pltpu.VMEM((count_y, coarse_own, width), f32),
            pltpu.VMEM(own.shape, bf16),
            pltpu.VMEM(coarse_in.shape, bf16),
            pltpu.VMEM(coarse_out.shape, bf16),
            pltpu.VMEM(edge_in.shape[1:], bf16),
            pltpu.VMEM(edge_in.shape[1:], bf16),
            pltpu.VMEM(edges.shape, bf16),
            pltpu.VMEM(edges.shape, bf16),
            pltpu.VMEM((rows_x * rows_y, blk, width), bf16),
            pltpu.VMEM(((rows_x + 2) * (rows_y + 2) * blk, 4, 128), f32),
            pltpu.VMEM((2, 32, 4, 8, 128), f32),
            pltpu.VMEM((33, 8, 128), f32),
            dma((5,)),
            dma((chunks,)),
            dma((chunks,)),
            dma((2, 3)),
            dma((2, 3)),
            dma((2,)),
            dma((2,)),
            dma((2, 2)),
            dma((2, 2)),
            dma((count_x,)),
            dma((count_x,)),
            dma((count_y,)),
            dma((count_y,)),
            dma((count_x,)),
            dma((count_x,)),
            dma((count_y,)),
            dma((count_y,)),
        ],
        compiler_params=pltpu.CompilerParams(
            collective_id=0, has_side_effects=True, vmem_limit_bytes=VMEM
        ),
        name="exchange",
    )(
        own,
        middle,
        row(parents),
        row(weights),
        row(mid_parents),
        row(mid_weights),
        coarse,
        coarse_in,
        row(bias),
        coarse_out,
        row(bias_two),
        row(gain),
        edges,
        edge_in,
        tb,
        tgt,
        src,
        src.reshape(-1),
        tb,
    )


def edge_kernel(
    shape,
    tb_ref,
    live_ref,
    tgt_ref,
    bias_ref,
    bias_two_ref,
    gain_ref,
    parent_ref,
    weight_ref,
    mid_ref,
    mid_parent_ref,
    mid_weight_ref,
    coarse_ref,
    coarse_own_ref,
    node_bias_ref,
    node_bias_two_ref,
    node_gain_ref,
    own_hbm,
    window_hbm,
    edge_in_hbm,
    wout_hbm,
    node_in_hbm,
    node_out_hbm,
    index_hbm,
    pre_hbm,
    edges_hbm,
    out_hbm,
    fine_hbm,
    mid_out_ref,
    coarse_out_ref,
    table,
    bufs,
    made_out,
    total,
    own_v,
    window_v,
    source_w,
    wout_v,
    node_in_v,
    node_out_v,
    bias_two_c,
    node_bias_two_c,
    doubled,
    pre_v,
    edges_v,
    index_first,
    index_even,
    index_odd,
    load_sem,
    index_sem,
    pre_sem,
    edge_sem,
    out_sem,
    fine_sem,
):
    rows_x, rows_y, blk, width = shape
    parts = width // LANES
    chunks = pre_sem.shape[0]
    chunk_rows = UNITS * blk
    rows = PAIR * blk
    per_chunk = UNITS // PAIR
    units = chunks * per_chunk
    live = live_ref[0]
    mids = mid_ref.shape[0]
    copy = pltpu.make_async_copy

    loads = [
        copy(edge_in_hbm.at[1], source_w, load_sem.at[0]),
        copy(own_hbm, own_v, load_sem.at[1]),
        copy(window_hbm, window_v, load_sem.at[2]),
        copy(wout_hbm, wout_v, load_sem.at[3]),
        copy(index_hbm.at[pl.ds(0, AHEAD * rows)], index_first, load_sem.at[4]),
        copy(node_in_hbm, node_in_v, load_sem.at[5]),
        copy(node_out_hbm, node_out_v, load_sem.at[6]),
    ]

    def chunk_at(c):
        return pl.ds(pl.multiple_of(c * chunk_rows, chunk_rows), chunk_rows)

    def pre_load(c):
        return copy(pre_hbm.at[chunk_at(c)], pre_v.at[chunk_at(c)], pre_sem.at[c])

    def edge_load(c):
        return copy(edges_hbm.at[chunk_at(c)], edges_v.at[chunk_at(c)], edge_sem.at[c])

    def out_store(c):
        return copy(edges_v.at[chunk_at(c)], out_hbm.at[chunk_at(c)], out_sem.at[c])

    def index_load(c, half):
        at = pl.ds(pl.multiple_of(c * chunk_rows + AHEAD * rows, rows), chunk_rows)
        return copy(index_hbm.at[at], (index_even, index_odd)[half], index_sem.at[half])

    def gather(index, first, slot):
        for e in range(rows):
            at = (e // 8) * (8 * parts) + e % 8
            row = pl.multiple_of(index[first + e], parts)
            bufs[slot, pl.ds(at, parts, stride=8), :] = table[pl.ds(row, parts), :]

    def second(number, slot, side):
        found = bufs[slot].reshape(rows // 8, parts, 8, LANES)
        found = jnp.concatenate([found[:, c].reshape(rows, LANES) for c in range(parts)], axis=1)
        at = pl.ds(pl.multiple_of(number * rows, rows), rows)
        hidden = activate(pre_v[at, :].astype(f32) + found).astype(bf16)
        made_out[side] = jnp.dot(hidden, wout_v[...], preferred_element_type=f32) + bias_two_c[...]

    def finish(number, side):
        for k in range(PAIR):
            block = number * PAIR + k
            centred = made_out[side, pl.ds(k * blk, blk), :]
            alive = (block < live).astype(f32)
            spread = jnp.mean(centred * centred, axis=-1, keepdims=True)
            message = (centred * (lax.rsqrt(spread + epsilon) * alive) * gain_ref[...]).astype(bf16)
            at = pl.ds(pl.multiple_of(block * blk, blk), blk)
            edges_v[at, :] = edges_v[at, :] + message
            target = tgt_ref[pl.ds(block, 1), :]
            pick = (lax.broadcasted_iota(jnp.int32, (blk, blk), 0) == target).astype(f32).astype(bf16)
            here = pl.multiple_of(tb_ref[block] * blk, blk)
            total[pl.ds(here, blk), :] += jnp.dot(pick, message, preferred_element_type=f32)

    for load in loads[:5]:
        load.start()
    for half in range(2):
        index_load(half, half).start()
    total[...] = jnp.zeros_like(total)
    coarse_out_ref[...] = coarse_own_ref[...]
    bias_two = bias_two_ref[...]
    bias_two_c[...] = bias_two - jnp.mean(bias_two, axis=-1, keepdims=True)
    bias_two = node_bias_two_ref[...]
    node_bias_two_c[...] = bias_two - jnp.mean(bias_two, axis=-1, keepdims=True)

    coarse = coarse_ref[...]
    ids = lax.broadcasted_iota(jnp.int32, (coarse.shape[0], mids), 0)
    high, low = split_two(jnp.where(ids == mid_parent_ref[...], mid_weight_ref[...], 0.0))
    value = mid_ref[...].astype(f32) + first_dims(high, coarse) + first_dims(low, coarse)
    value = value.astype(bf16)
    mid_out_ref[...] = value
    doubled[pl.ds(0, mids), :] = value
    doubled[pl.ds(mids, mids), :] = value

    def fill(places, block_rows):
        made = jnp.dot(block_rows, source_w[...], preferred_element_type=f32)
        made = (made + bias_ref[...]) * 0.5
        for k, (a, b) in enumerate(places):
            number = a * (rows_y + 2) + b
            for c in range(parts):
                at = pl.ds(number * blk * parts + c, blk, stride=parts)
                table[at, :] = made[k * blk : (k + 1) * blk, c * LANES : (c + 1) * LANES]

    loads[0].wait()
    loads[1].wait()
    inner = [(a, b) for a in range(1, rows_x + 1) for b in range(1, rows_y + 1)]
    fill(inner, own_v[...].reshape(len(inner) * blk, width))
    loads[2].wait()
    for c in range(2):
        pre_load(c).start()
        edge_load(c).start()
    for a in (0, rows_x + 1):
        fill([(a, b) for b in range(rows_y + 2)], window_v[a].reshape((rows_y + 2) * blk, width))
    for b in (0, rows_y + 1):
        fill([(a, b) for a in range(1, rows_x + 1)], window_v[1 : rows_x + 1, b].reshape(rows_x * blk, width))
    loads[3].wait()
    wout_v[...] = centred_rows(wout_v[...])
    loads[4].wait()
    for u in range(AHEAD):
        gather(index_first, u * rows, u % SLOTS)
    pre_load(0).wait()
    second(0, 0, 0)
    for load in loads[5:]:
        load.start()

    def half_step(c, half):
        edge_load(c).wait()
        index_load(c, half).wait()

        @pl.when(c + 2 < chunks)
        def _():
            pre_load(c + 2).start()
            edge_load(c + 2).start()

        @pl.when(c + 1 < chunks)
        def _():
            pre_load(c + 1).wait()

        @pl.when(c * UNITS < live)
        def _():
            for u in range(per_chunk):
                number = c * per_chunk + u
                gather((index_even, index_odd)[half], u * rows, (u + AHEAD) % SLOTS)
                second(jnp.minimum(number + 1, units - 1), (u + 1) % SLOTS, (u + 1) % 2)
                finish(number, u % 2)

        out_store(c).start()

        @pl.when(c + 2 < chunks)
        def _():
            index_load(c + 2, half).start()

    def two_steps(i, carry):
        half_step(2 * i, 0)
        half_step(2 * i + 1, 1)
        return carry

    lax.fori_loop(0, chunks // 2, two_steps, 0)

    loads[5].wait()
    loads[6].wait()
    node_out_v[...] = centred_rows(node_out_v[...])
    wide = rows_y * blk
    for a in range(rows_x):
        at = pl.ds(a * wide, wide)
        own = own_v[a].reshape(wide, width)
        pre = jnp.dot(own, node_in_v[0], preferred_element_type=f32)
        pre = pre + jnp.dot(total[at, :].astype(bf16), node_in_v[1], preferred_element_type=f32)
        hidden = activate((pre + node_bias_ref[...]) * 0.5).astype(bf16)
        centred = jnp.dot(hidden, node_out_v[...], preferred_element_type=f32) + node_bias_two_c[...]
        fine = own.astype(f32) + norm_centred(centred, node_gain_ref[...])
        ids = lax.broadcasted_iota(jnp.int32, (mids, wide), 0)
        high, low = split_two(jnp.where(ids == parent_ref[:, at], weight_ref[:, at], 0.0))
        from_middle = first_dims(jnp.concatenate([high, low], axis=0), doubled[...])
        own_v[a] = (fine + from_middle).astype(bf16).reshape(own_v.shape[1:])
        copy(own_v.at[a], fine_hbm.at[a], fine_sem.at[a]).start()
    for a in range(rows_x):
        copy(own_v.at[a], fine_hbm.at[a], fine_sem.at[a]).wait()
    for c in range(chunks):
        out_store(c).wait()


def run_edges(own, window, pre, edges, index, block_target, node_target, live, edge_params, nodes, node_params):
    rows_x, rows_y, blk, width = own.shape
    edge_in, bias, edge_out, bias_two, gain = edge_params
    node_in, node_bias, node_out, node_bias_two, node_gain = node_params
    parents, weights, middle, mid_parents, mid_weights, coarse, coarse_own = nodes
    chunks = edges.shape[0] // (UNITS * blk)
    row = lambda array: array.reshape(1, -1)
    own_count = rows_x * rows_y * blk
    hbm = pl.BlockSpec(memory_space=pl.ANY)
    vmem = pl.BlockSpec(memory_space=pltpu.VMEM)
    smem = pl.BlockSpec(memory_space=pltpu.SMEM)
    dma = pltpu.SemaphoreType.DMA
    small = [node_target, row(bias), row(bias_two), row(gain), row(parents), row(weights), middle]
    small += [row(mid_parents), row(mid_weights), coarse, coarse_own]
    small += [row(node_bias), row(node_bias_two), row(node_gain)]
    large = [own, window, edge_in, edge_out, node_in, node_out, index.reshape(-1), pre, edges]
    return pl.pallas_call(
        functools.partial(edge_kernel, own.shape),
        in_specs=[smem] * 2 + [vmem] * len(small) + [hbm] * len(large),
        out_specs=[hbm, hbm, vmem, vmem],
        scratch_shapes=[
            pltpu.VMEM(((rows_x + 2) * (rows_y + 2) * blk * (width // LANES), LANES), f32),
            pltpu.VMEM((SLOTS, PAIR * blk * width // LANES, LANES), f32),
            pltpu.VMEM((2, PAIR * blk, width), f32),
            pltpu.VMEM((own_count, width), f32),
            pltpu.VMEM(own.shape, bf16),
            pltpu.VMEM(window.shape, bf16),
            pltpu.VMEM(edge_in.shape[1:], bf16),
            pltpu.VMEM(edge_out.shape, bf16),
            pltpu.VMEM(node_in.shape, bf16),
            pltpu.VMEM(node_out.shape, bf16),
            pltpu.VMEM((1, width), f32),
            pltpu.VMEM((1, width), f32),
            pltpu.VMEM((2 * middle.shape[0], width), bf16),
            pltpu.VMEM(edges.shape, bf16),
            pltpu.VMEM(edges.shape, bf16),
            pltpu.SMEM((AHEAD * PAIR * blk,), jnp.int32),
            pltpu.SMEM((UNITS * blk,), jnp.int32),
            pltpu.SMEM((UNITS * blk,), jnp.int32),
            dma((7,)),
            dma((2,)),
            dma((chunks,)),
            dma((chunks,)),
            dma((chunks,)),
            dma((rows_x,)),
        ],
        out_shape=[
            jax.ShapeDtypeStruct(edges.shape, bf16),
            jax.ShapeDtypeStruct(own.shape, bf16),
            jax.ShapeDtypeStruct(middle.shape, bf16),
            jax.ShapeDtypeStruct(coarse_own.shape, bf16),
        ],
        compiler_params=pltpu.CompilerParams(vmem_limit_bytes=VMEM),
        name="edge_node_layer",
    )(block_target, live.reshape(1), *small, *large)


def body(
    fine_nodes,
    edge_states,
    middle_nodes,
    coarse_nodes,
    edge_sources,
    target_blocks,
    target_nodes,
    live_blocks,
    fine_parent,
    fine_weight,
    middle_parent,
    middle_weight,
    edge_in,
    edge_bias,
    edge_out,
    edge_bias_two,
    edge_gain,
    node_in,
    node_bias,
    node_out,
    node_bias_two,
    node_gain,
    coarse_in,
    coarse_bias,
    coarse_out,
    coarse_bias_two,
    coarse_gain,
):
    rows_x, rows_y, block_size, latent = fine_nodes.shape
    own_count = rows_x * rows_y * block_size
    edge_params = (edge_in, edge_bias, edge_out, edge_bias_two, edge_gain)
    node_params = (node_in, node_bias, node_out, node_bias_two, node_gain)
    parents_local = fine_parent.reshape(own_count)
    weights_local = fine_weight.reshape(own_count)
    middle_rows = middle_nodes[0, 0]
    mid_parents = middle_parent[0, 0]
    mid_weights = middle_weight[0, 0]
    coarse_own = coarse_nodes.shape[0]
    devices = lax.axis_size(("gx", "gy"))
    edges = edge_states.reshape(-1, latent)
    window, everyone, coarse_own_rows, middle_mid, pre, index = exchange(
        fine_nodes,
        middle_rows,
        parents_local,
        weights_local,
        mid_parents,
        mid_weights,
        coarse_nodes,
        (coarse_in, coarse_bias, coarse_out, coarse_bias_two, coarse_gain),
        edges,
        edge_in,
        target_blocks[0, 0],
        target_nodes[0, 0],
        edge_sources[0, 0],
    )
    everyone = everyone.reshape(devices * coarse_own, latent)
    nodes = (parents_local, weights_local, middle_mid, mid_parents, mid_weights, everyone, coarse_own_rows)
    edge_result, fine_result, middle_result, coarse_result = run_edges(
        fine_nodes,
        window,
        pre,
        edges,
        index,
        target_blocks[0, 0],
        target_nodes[0, 0],
        live_blocks[0, 0],
        edge_params,
        nodes,
        node_params,
    )
    return (
        fine_result.reshape(fine_nodes.shape),
        edge_result.reshape(edge_states.shape),
        middle_result.reshape(middle_nodes.shape),
        coarse_result,
    )


def solution(mesh):
    placed = (
        P("gx", "gy", None, None),
        P("gx", "gy", None, None, None),
        P("gx", "gy", None, None),
        P(("gx", "gy"), None),
        P("gx", "gy", None, None),
        P("gx", "gy", None),
        P("gx", "gy", None, None),
        P("gx", "gy"),
        P("gx", "gy", None),
        P("gx", "gy", None),
        P("gx", "gy", None),
        P("gx", "gy", None),
        P(),
        P(),
        P(),
        P(),
        P(),
        P(),
        P(),
        P(),
        P(),
        P(),
        P(),
        P(),
        P(),
        P(),
        P(),
    )
    return jax.shard_map(
        body,
        mesh=mesh,
        in_specs=placed,
        out_specs=(
            P("gx", "gy", None, None),
            P("gx", "gy", None, None, None),
            P("gx", "gy", None, None),
            P(("gx", "gy"), None),
        ),
        check_vma=False,
    )
```

```python
import functools

import jax
import jax.numpy as jnp
from jax import lax
from jax.experimental import pallas as pl
from jax.experimental.pallas import tpu as pltpu
from jax.sharding import PartitionSpec as P

epsilon = 1e-05
f32 = jnp.float32
bf16 = jnp.bfloat16
GROUP = 4
UNITS = 8
PAIR = 2
AHEAD = 2
SLOTS = 4
LANES = 128
VMEM = 64 * 1024 * 1024


def layer_norm(values, gain_vec):
    centred = values - jnp.mean(values, axis=-1, keepdims=True)
    spread = jnp.mean(centred * centred, axis=-1, keepdims=True)
    return centred * lax.rsqrt(spread + epsilon) * gain_vec


def first_dims(left, right):
    return lax.dot_general(left, right, (((0,), (0,)), ((), ())), preferred_element_type=f32)


def split_two(values):
    high = values.astype(bf16)
    return high, (values - high.astype(f32)).astype(bf16)


def activate(half):
    return half + half * jnp.tanh(half)


def centred_rows(weights):
    wide = weights.astype(f32)
    return (wide - jnp.mean(wide, axis=-1, keepdims=True)).astype(bf16)


def norm_centred(centred, gain_vec):
    spread = jnp.mean(centred * centred, axis=-1, keepdims=True)
    return centred * lax.rsqrt(spread + epsilon) * gain_vec


def exchange_kernel(
    grid_shape,
    own_hbm,
    mid_ref,
    parent_ref,
    weight_ref,
    mid_parent_ref,
    mid_weight_ref,
    coarse_ref,
    win_hbm,
    bias_ref,
    wout_hbm,
    bias_two_ref,
    gain_ref,
    edges_hbm,
    edge_in_hbm,
    tb_ref,
    tgt_ref,
    src_ref,
    edge_bias_ref,
    everyone_ref,
    result_ref,
    middle_ref,
    pre_hbm,
    table_hbm,
    index_ref,
    partial,
    arrived_x,
    summed_x,
    arrived_y,
    own_v,
    win_v,
    wout_v,
    first_w,
    target_w,
    edges_v,
    pre_v,
    target_table,
    window_ref,
    source_w,
    table,
    load_sem,
    table_store,
    edge_load,
    pre_store,
    side_send,
    side_recv,
    edge_send,
    edge_recv,
    corner_send,
    corner_recv,
    sx_send,
    sx_recv,
    sy_send,
    sy_recv,
    gx_send,
    gx_recv,
    gy_send,
    gy_recv,
):
    count_x, count_y = grid_shape
    rows_x, rows_y, blk, width = own_hbm.shape
    mids = mid_ref.shape[0]
    parts = width // LANES
    chunks = edge_load.shape[0]
    chunk_rows = edges_v.shape[0] // chunks
    at_x, at_y = lax.axis_index("gx"), lax.axis_index("gy")
    peers_x = [lax.rem(at_x + offset, count_x) for offset in range(1, count_x)]
    peers_y = [lax.rem(at_y + offset, count_y) for offset in range(1, count_y)]
    mesh_ids = pl.DeviceIdType.MESH

    barrier = pltpu.get_barrier_semaphore()
    for x in peers_x:
        pl.semaphore_signal(barrier, inc=1, device_id=(x, at_y), device_id_type=mesh_ids)
    for y in peers_y:
        pl.semaphore_signal(barrier, inc=1, device_id=(at_x, y), device_id_type=mesh_ids)

    loads = [
        pltpu.make_async_copy(own_hbm, own_v, load_sem.at[0]),
        pltpu.make_async_copy(edge_in_hbm.at[2], target_w, load_sem.at[1]),
        pltpu.make_async_copy(edge_in_hbm.at[0], first_w, load_sem.at[2]),
        pltpu.make_async_copy(edge_in_hbm.at[1], source_w, load_sem.at[3]),
        pltpu.make_async_copy(win_hbm, win_v, load_sem.at[4]),
        pltpu.make_async_copy(wout_hbm, wout_v, load_sem.at[5]),
    ]

    def edge_chunk(i):
        rows = pl.ds(i * chunk_rows, chunk_rows)
        return pltpu.make_async_copy(edges_hbm.at[rows], edges_v.at[rows], edge_load.at[i])

    def pre_chunk(i):
        rows = pl.ds(i * chunk_rows, chunk_rows)
        return pltpu.make_async_copy(pre_v.at[rows], pre_hbm.at[rows], pre_store.at[i])

    for load in loads[:3]:
        load.start()
    blocks = src_ref.shape[0]
    index_ref[pl.ds(0, blocks), :] = src_ref[...] * (width // LANES)
    extra = index_ref.shape[0] - blocks
    index_ref[pl.ds(blocks, extra), :] = jnp.zeros((extra, blk), jnp.int32)
    pl.semaphore_wait(barrier, count_x + count_y - 2)

    def remote(src, dst, send, recv, x, y):
        return pltpu.make_async_remote_copy(
            src_ref=src,
            dst_ref=dst,
            send_sem=send,
            recv_sem=recv,
            device_id=(x, y),
            device_id_type=mesh_ids,
        )

    def has_x(x):
        return (x >= 0) & (x < count_x)

    def has_y(y):
        return (y >= 0) & (y < count_y)

    pieces = [(0, 1), (rows_x - 1, 1)] + ([(1, rows_x - 2)] if rows_x > 2 else [])
    ways = [1, -1]

    def side_copy(way, piece, y):
        first, length = pieces[piece]
        column = rows_y - 1 if ways[way] == 1 else 0
        to = 0 if ways[way] == 1 else rows_y + 1
        return remote(
            own_hbm.at[pl.ds(first, length), pl.ds(column, 1)],
            window_ref.at[pl.ds(first + 1, length), pl.ds(to, 1)],
            side_send.at[way, piece],
            side_recv.at[way, piece],
            at_x,
            y,
        )

    def edge_copy(way, x):
        row = rows_x - 1 if ways[way] == 1 else 0
        to = 0 if ways[way] == 1 else rows_x + 1
        return remote(
            own_hbm.at[row], window_ref.at[to, pl.ds(1, rows_y)], edge_send.at[way], edge_recv.at[way], x, at_y
        )

    def corner_copy(way, side, x):
        row = rows_x if ways[way] == 1 else 1
        to = 0 if ways[way] == 1 else rows_x + 1
        column = 0 if ways[side] == 1 else rows_y + 1
        return remote(
            window_ref.at[row, column],
            window_ref.at[to, column],
            corner_send.at[way, side],
            corner_recv.at[way, side],
            x,
            at_y,
        )

    def start_sides(piece):
        for way in range(2):

            @pl.when(has_y(at_y + ways[way]))
            def _():
                side_copy(way, piece, at_y + ways[way]).start()

    def sum_x_copy(slot_from, slot_to, x):
        return remote(
            partial.at[slot_from], arrived_x.at[slot_to], sx_send.at[slot_from], sx_recv.at[slot_to], x, at_y
        )

    def sum_y_copy(slot_from, slot_to, y):
        return remote(
            summed_x.at[slot_from], arrived_y.at[slot_to], sy_send.at[slot_from], sy_recv.at[slot_to], at_x, y
        )

    def full_y_copy(slot, y):
        here = everyone_ref.at[at_x, slot]
        return remote(here, here, gy_send.at[y], gy_recv.at[slot], at_x, y)

    def full_x_copy(slot, x):
        here = everyone_ref.at[slot]
        return remote(here, here, gx_send.at[x], gx_recv.at[slot], x, at_y)

    start_sides(0)
    start_sides(1)
    loads[0].wait()
    for i in range(chunks):
        edge_chunk(i).start()
    for load in loads[3:]:
        load.start()
    own = own_v[...].reshape(rows_x * rows_y * blk, width)
    ids = lax.broadcasted_iota(jnp.int32, (mids, own.shape[0]), 0)
    high, low = split_two(jnp.where(ids == parent_ref[...], weight_ref[...], 0.0))
    middle = mid_ref[...].astype(f32) + jnp.dot(high, own, preferred_element_type=f32)
    middle = (middle + jnp.dot(low, own, preferred_element_type=f32)).astype(bf16)
    ids = lax.broadcasted_iota(jnp.int32, (count_x * count_y * coarse_ref.shape[0], mids), 0)
    high, low = split_two(jnp.where(ids == mid_parent_ref[...], mid_weight_ref[...], 0.0))
    sums = jnp.dot(high, middle, preferred_element_type=f32)
    sums = sums + jnp.dot(low, middle, preferred_element_type=f32)
    partial[...] = sums.reshape(partial.shape).astype(bf16)
    middle_ref[...] = middle

    for x in peers_x:
        sum_x_copy(x, at_x, x).start()

    loads[1].wait()
    made = jnp.dot(own, target_w[...], preferred_element_type=f32) * 0.5
    target_table[...] = made.astype(bf16).reshape(target_table.shape)
    loads[2].wait()
    first_w[...] = first_w[...] * 0.5

    per_row = (rows_y + 2) * blk * parts

    def fill(places, block_rows):
        made = jnp.dot(block_rows, source_w[...], preferred_element_type=f32)
        made = (made + edge_bias_ref[...]) * 0.5
        for k, (a, b) in enumerate(places):
            number = a * (rows_y + 2) + b
            for c in range(parts):
                at = pl.ds(number * blk * parts + c, blk, stride=parts)
                table[at, :] = made[k * blk : (k + 1) * blk, c * LANES : (c + 1) * LANES]

    def table_copy(a):
        at = pl.ds(a * per_row, per_row)
        return pltpu.make_async_copy(table.at[at], table_hbm.at[at], table_store.at[a])

    rows = GROUP * blk

    def group(g, carry):
        at = pl.ds(pl.multiple_of(g * rows, rows), rows)
        from_target = []
        for k in range(GROUP):
            number = g * GROUP + k
            target = tgt_ref[pl.ds(number, 1), :]
            pick = (lax.broadcasted_iota(jnp.int32, (blk, blk), 0) == target).astype(f32).astype(bf16)
            from_target.append(first_dims(pick, target_table[tb_ref[number]]))
        made = jnp.dot(edges_v[at, :], first_w[...], preferred_element_type=f32)
        pre_v[at, :] = (made + jnp.concatenate(from_target, axis=0)).astype(bf16)
        return carry

    def work(first, last):
        for i in range(first, last):
            edge_chunk(i).wait()
        lax.fori_loop(first * (chunk_rows // rows), last * (chunk_rows // rows), group, 0)
        for i in range(first, last):
            pre_chunk(i).start()

    marks = [(chunks * part) // 8 for part in range(9)]

    work(marks[0], marks[3])

    total = partial[at_x].astype(f32)
    for x in peers_x:
        sum_x_copy(x, x, x).wait_recv()
        total = total + arrived_x[x].astype(f32)
    summed_x[...] = total
    for y in peers_y:
        sum_y_copy(y, at_y, y).start()
    for way in range(2):

        @pl.when(has_x(at_x + ways[way]))
        def _():
            edge_copy(way, at_x + ways[way]).start()

    work(marks[3], marks[5])

    for side in range(2):
        from_y = at_y - ways[side]

        @pl.when(has_y(from_y))
        def _():
            side_copy(side, 0, from_y).wait_recv()
            side_copy(side, 1, from_y).wait_recv()
            for way in range(2):

                @pl.when(has_x(at_x + ways[way]))
                def _():
                    corner_copy(way, side, at_x + ways[way]).start()

    restricted = summed_x[at_y]
    for y in peers_y:
        sum_y_copy(y, y, y).wait_recv()
        restricted = restricted + arrived_y[y]
    if len(pieces) > 2:
        start_sides(2)

    loads[4].wait()
    loads[5].wait()
    coarse = coarse_ref[...]
    pre = jnp.dot(coarse, win_v[0], preferred_element_type=f32)
    pre = pre + jnp.dot(restricted.astype(bf16), win_v[1], preferred_element_type=f32)
    hidden = activate((pre + bias_ref[...]) * 0.5).astype(bf16)
    output = jnp.dot(hidden, wout_v[...], preferred_element_type=f32) + bias_two_ref[...]
    result = (coarse.astype(f32) + layer_norm(output, gain_ref[...])).astype(bf16)
    everyone_ref[at_x, at_y] = result
    result_ref[...] = result
    for y in peers_y:
        full_y_copy(at_y, y).start()

    work(marks[5], marks[7])

    for y in peers_y:
        full_y_copy(y, y).wait_recv()
    for x in peers_x:
        full_x_copy(at_x, x).start()

    work(marks[7], marks[8])

    loads[3].wait()
    fill([(a, b) for a in range(1, rows_x + 1) for b in range(1, rows_y + 1)], own)

    for way in range(2):

        @pl.when(has_x(at_x - ways[way]))
        def _():
            edge_copy(way, at_x - ways[way]).wait_recv()

        @pl.when(has_x(at_x + ways[way]))
        def _():
            edge_copy(way, at_x + ways[way]).wait_send()

        @pl.when(has_y(at_y + ways[way]))
        def _():
            for piece in range(len(pieces)):
                side_copy(way, piece, at_y + ways[way]).wait_send()

        if len(pieces) > 2:

            @pl.when(has_y(at_y - ways[way]))
            def _():
                side_copy(way, 2, at_y - ways[way]).wait_recv()

        for side in range(2):

            @pl.when(has_y(at_y - ways[side]) & has_x(at_x + ways[way]))
            def _():
                corner_copy(way, side, at_x + ways[way]).wait_send()

            @pl.when(has_y(at_y - ways[side]) & has_x(at_x - ways[way]))
            def _():
                corner_copy(way, side, at_x - ways[way]).wait_recv()

    for b in (0, rows_y + 1):
        fill([(a, b) for a in range(1, rows_x + 1)], window_ref[1 : rows_x + 1, b].reshape(rows_x * blk, width))
    for a in range(1, rows_x + 1):
        table_copy(a).start()
    for a in (0, rows_x + 1):
        fill([(a, b) for b in range(rows_y + 2)], window_ref[a].reshape((rows_y + 2) * blk, width))
        table_copy(a).start()

    for x in peers_x:
        sum_x_copy(x, at_x, x).wait_send()
        full_x_copy(at_x, x).wait_send()
        full_x_copy(x, x).wait_recv()
    for y in peers_y:
        sum_y_copy(y, at_y, y).wait_send()
        full_y_copy(at_y, y).wait_send()
    for i in range(chunks):
        pre_chunk(i).wait()
    for a in range(rows_x + 2):
        table_copy(a).wait()


def exchange(own, middle, parents, weights, mid_parents, mid_weights, coarse, params, edges, edge_params, tb, tgt, src):
    rows_x, rows_y, blk, width = own.shape
    count_x, count_y = lax.axis_size("gx"), lax.axis_size("gy")
    coarse_own = coarse.shape[0]
    coarse_in, bias, coarse_out, bias_two, gain = params
    edge_in, edge_bias = edge_params
    table_shape = ((rows_x + 2) * (rows_y + 2) * blk * (width // LANES), LANES)
    row = lambda array: array.reshape(1, -1)
    vmem = pl.BlockSpec(memory_space=pltpu.VMEM)
    smem = pl.BlockSpec(memory_space=pltpu.SMEM)
    hbm = pl.BlockSpec(memory_space=pl.ANY)
    dma = pltpu.SemaphoreType.DMA
    chunks = src.shape[0] // UNITS
    return pl.pallas_call(
        functools.partial(exchange_kernel, (count_x, count_y)),
        in_specs=[hbm] + [vmem] * 6 + [hbm, vmem, hbm, vmem, vmem, hbm, hbm, smem, vmem, vmem, vmem],
        out_specs=[vmem, vmem, vmem, hbm, hbm, vmem],
        out_shape=[
            jax.ShapeDtypeStruct((count_x, count_y, coarse_own, width), bf16),
            jax.ShapeDtypeStruct((coarse_own, width), bf16),
            jax.ShapeDtypeStruct(middle.shape, bf16),
            jax.ShapeDtypeStruct(edges.shape, bf16),
            jax.ShapeDtypeStruct(table_shape, f32),
            jax.ShapeDtypeStruct((src.shape[0] + UNITS, blk), jnp.int32),
        ],
        scratch_shapes=[
            pltpu.VMEM((count_x, count_y, coarse_own, width), bf16),
            pltpu.VMEM((count_x, count_y, coarse_own, width), bf16),
            pltpu.VMEM((count_y, coarse_own, width), f32),
            pltpu.VMEM((count_y, coarse_own, width), f32),
            pltpu.VMEM(own.shape, bf16),
            pltpu.VMEM(coarse_in.shape, bf16),
            pltpu.VMEM(coarse_out.shape, bf16),
            pltpu.VMEM(edge_in.shape[1:], bf16),
            pltpu.VMEM(edge_in.shape[1:], bf16),
            pltpu.VMEM(edges.shape, bf16),
            pltpu.VMEM(edges.shape, bf16),
            pltpu.VMEM((rows_x * rows_y, blk, width), bf16),
            pltpu.VMEM((rows_x + 2, rows_y + 2, blk, width), bf16),
            pltpu.VMEM(edge_in.shape[1:], bf16),
            pltpu.VMEM(table_shape, f32),
            dma((6,)),
            dma((rows_x + 2,)),
            dma((chunks,)),
            dma((chunks,)),
            dma((2, 3)),
            dma((2, 3)),
            dma((2,)),
            dma((2,)),
            dma((2, 2)),
            dma((2, 2)),
            dma((count_x,)),
            dma((count_x,)),
            dma((count_y,)),
            dma((count_y,)),
            dma((count_x,)),
            dma((count_x,)),
            dma((count_y,)),
            dma((count_y,)),
        ],
        compiler_params=pltpu.CompilerParams(
            collective_id=0, has_side_effects=True, vmem_limit_bytes=VMEM
        ),
        name="exchange",
    )(
        own,
        middle,
        row(parents),
        row(weights),
        row(mid_parents),
        row(mid_weights),
        coarse,
        coarse_in,
        row(bias),
        coarse_out,
        row(bias_two),
        row(gain),
        edges,
        edge_in,
        tb,
        tgt,
        src,
        row(edge_bias),
    )


def edge_kernel(
    shape,
    tb_ref,
    live_ref,
    tgt_ref,
    bias_two_ref,
    gain_ref,
    parent_ref,
    weight_ref,
    mid_ref,
    mid_parent_ref,
    mid_weight_ref,
    coarse_ref,
    coarse_own_ref,
    node_bias_ref,
    node_bias_two_ref,
    node_gain_ref,
    own_hbm,
    table_hbm,
    wout_hbm,
    node_in_hbm,
    node_out_hbm,
    index_hbm,
    pre_hbm,
    edges_hbm,
    out_hbm,
    fine_hbm,
    mid_out_ref,
    coarse_out_ref,
    table,
    bufs,
    made_out,
    total,
    own_v,
    wout_v,
    node_in_v,
    node_out_v,
    bias_two_c,
    node_bias_two_c,
    doubled,
    node_pre,
    fine_base,
    pre_v,
    edges_v,
    index_first,
    index_even,
    index_odd,
    load_sem,
    index_sem,
    pre_sem,
    edge_sem,
    out_sem,
    fine_sem,
):
    rows_x, rows_y, blk, width = shape
    parts = width // LANES
    chunks = pre_sem.shape[0]
    chunk_rows = UNITS * blk
    rows = PAIR * blk
    per_chunk = UNITS // PAIR
    units = chunks * per_chunk
    live = live_ref[0]
    mids = mid_ref.shape[0]
    copy = pltpu.make_async_copy

    loads = [
        copy(table_hbm, table, load_sem.at[1]),
        copy(wout_hbm, wout_v, load_sem.at[0]),
        copy(index_hbm.at[pl.ds(0, AHEAD * rows)], index_first, load_sem.at[2]),
        copy(own_hbm, own_v, load_sem.at[3]),
        copy(node_in_hbm, node_in_v, load_sem.at[4]),
        copy(node_out_hbm, node_out_v, load_sem.at[5]),
    ]

    def chunk_at(c):
        return pl.ds(pl.multiple_of(c * chunk_rows, chunk_rows), chunk_rows)

    def pre_load(c):
        return copy(pre_hbm.at[chunk_at(c)], pre_v.at[chunk_at(c)], pre_sem.at[c])

    def edge_load(c):
        return copy(edges_hbm.at[chunk_at(c)], edges_v.at[chunk_at(c)], edge_sem.at[c])

    def out_store(c):
        return copy(edges_v.at[chunk_at(c)], out_hbm.at[chunk_at(c)], out_sem.at[c])

    def index_load(c, half):
        at = pl.ds(pl.multiple_of(c * chunk_rows + AHEAD * rows, rows), chunk_rows)
        return copy(index_hbm.at[at], (index_even, index_odd)[half], index_sem.at[half])

    def gather(index, first, slot):
        for e in range(rows):
            at = (e // 8) * (8 * parts) + e % 8
            row = pl.multiple_of(index[first + e], parts)
            bufs[slot, pl.ds(at, parts, stride=8), :] = table[pl.ds(row, parts), :]

    def second(number, slot, side):
        found = bufs[slot].reshape(rows // 8, parts, 8, LANES)
        found = jnp.concatenate([found[:, c].reshape(rows, LANES) for c in range(parts)], axis=1)
        at = pl.ds(pl.multiple_of(number * rows, rows), rows)
        hidden = activate(pre_v[at, :].astype(f32) + found).astype(bf16)
        made_out[side] = jnp.dot(hidden, wout_v[...], preferred_element_type=f32) + bias_two_c[...]

    def finish(number, side):
        for k in range(PAIR):
            block = number * PAIR + k
            centred = made_out[side, pl.ds(k * blk, blk), :]
            alive = (block < live).astype(f32)
            spread = jnp.mean(centred * centred, axis=-1, keepdims=True)
            message = (centred * (lax.rsqrt(spread + epsilon) * alive) * gain_ref[...]).astype(bf16)
            at = pl.ds(pl.multiple_of(block * blk, blk), blk)
            edges_v[at, :] = edges_v[at, :] + message
            target = tgt_ref[pl.ds(block, 1), :]
            pick = (lax.broadcasted_iota(jnp.int32, (blk, blk), 0) == target).astype(f32).astype(bf16)
            here = pl.multiple_of(tb_ref[block] * blk, blk)
            total[pl.ds(here, blk), :] += jnp.dot(pick, message, preferred_element_type=f32)

    loads[3].start()
    loads[4].start()
    for load in loads[:3]:
        load.start()
    for half in range(2):
        index_load(half, half).start()
    for c in range(2):
        pre_load(c).start()
        edge_load(c).start()
    loads[5].start()
    total[...] = jnp.zeros_like(total)
    coarse_out_ref[...] = coarse_own_ref[...]
    bias_two = bias_two_ref[...]
    bias_two_c[...] = bias_two - jnp.mean(bias_two, axis=-1, keepdims=True)
    bias_two = node_bias_two_ref[...]
    node_bias_two_c[...] = bias_two - jnp.mean(bias_two, axis=-1, keepdims=True)

    coarse = coarse_ref[...]
    ids = lax.broadcasted_iota(jnp.int32, (coarse.shape[0], mids), 0)
    high, low = split_two(jnp.where(ids == mid_parent_ref[...], mid_weight_ref[...], 0.0))
    value = mid_ref[...].astype(f32) + first_dims(high, coarse) + first_dims(low, coarse)
    value = value.astype(bf16)
    mid_out_ref[...] = value
    doubled[pl.ds(0, mids), :] = value
    doubled[pl.ds(mids, mids), :] = value

    loads[3].wait()
    loads[4].wait()
    wide = rows_y * blk
    for a in range(rows_x):
        at = pl.ds(a * wide, wide)
        own = own_v[a].reshape(wide, width)
        node_pre[at, :] = jnp.dot(own, node_in_v[0], preferred_element_type=f32) + node_bias_ref[...]
        ids = lax.broadcasted_iota(jnp.int32, (mids, wide), 0)
        high, low = split_two(jnp.where(ids == parent_ref[:, at], weight_ref[:, at], 0.0))
        from_middle = first_dims(jnp.concatenate([high, low], axis=0), doubled[...])
        fine_base[at, :] = own.astype(f32) + from_middle
    loads[1].wait()
    wout_v[...] = centred_rows(wout_v[...])
    loads[0].wait()
    loads[2].wait()
    for u in range(AHEAD):
        gather(index_first, u * rows, u % SLOTS)
    pre_load(0).wait()
    second(0, 0, 0)

    def half_step(c, half):
        edge_load(c).wait()
        index_load(c, half).wait()

        @pl.when(c + 2 < chunks)
        def _():
            pre_load(c + 2).start()
            edge_load(c + 2).start()

        @pl.when(c + 1 < chunks)
        def _():
            pre_load(c + 1).wait()

        @pl.when(c * UNITS < live)
        def _():
            for u in range(per_chunk):
                number = c * per_chunk + u
                gather((index_even, index_odd)[half], u * rows, (u + AHEAD) % SLOTS)
                second(jnp.minimum(number + 1, units - 1), (u + 1) % SLOTS, (u + 1) % 2)
                finish(number, u % 2)

        out_store(c).start()

        @pl.when(c + 2 < chunks)
        def _():
            index_load(c + 2, half).start()

    def two_steps(i, carry):
        half_step(2 * i, 0)
        half_step(2 * i + 1, 1)
        return carry

    lax.fori_loop(0, chunks // 2, two_steps, 0)

    loads[5].wait()
    node_out_v[...] = centred_rows(node_out_v[...])
    for a in range(rows_x):
        at = pl.ds(a * wide, wide)
        pre = node_pre[at, :] + jnp.dot(total[at, :].astype(bf16), node_in_v[1], preferred_element_type=f32)
        hidden = activate(pre * 0.5).astype(bf16)
        centred = jnp.dot(hidden, node_out_v[...], preferred_element_type=f32) + node_bias_two_c[...]
        fine = fine_base[at, :] + norm_centred(centred, node_gain_ref[...])
        own_v[a] = fine.astype(bf16).reshape(own_v.shape[1:])
        copy(own_v.at[a], fine_hbm.at[a], fine_sem.at[a]).start()
    for a in range(rows_x):
        copy(own_v.at[a], fine_hbm.at[a], fine_sem.at[a]).wait()
    for c in range(chunks):
        out_store(c).wait()


def run_edges(own, table, pre, edges, index, block_target, node_target, live, edge_params, nodes, node_params):
    rows_x, rows_y, blk, width = own.shape
    edge_out, bias_two, gain = edge_params
    node_in, node_bias, node_out, node_bias_two, node_gain = node_params
    parents, weights, middle, mid_parents, mid_weights, coarse, coarse_own = nodes
    chunks = edges.shape[0] // (UNITS * blk)
    row = lambda array: array.reshape(1, -1)
    own_count = rows_x * rows_y * blk
    hbm = pl.BlockSpec(memory_space=pl.ANY)
    vmem = pl.BlockSpec(memory_space=pltpu.VMEM)
    smem = pl.BlockSpec(memory_space=pltpu.SMEM)
    dma = pltpu.SemaphoreType.DMA
    small = [node_target, row(bias_two), row(gain), row(parents), row(weights), middle]
    small += [row(mid_parents), row(mid_weights), coarse, coarse_own]
    small += [row(node_bias), row(node_bias_two), row(node_gain)]
    large = [own, table, edge_out, node_in, node_out, index.reshape(-1), pre, edges]
    return pl.pallas_call(
        functools.partial(edge_kernel, own.shape),
        in_specs=[smem] * 2 + [vmem] * len(small) + [hbm] * len(large),
        out_specs=[hbm, hbm, vmem, vmem],
        scratch_shapes=[
            pltpu.VMEM(table.shape, f32),
            pltpu.VMEM((SLOTS, PAIR * blk * width // LANES, LANES), f32),
            pltpu.VMEM((2, PAIR * blk, width), f32),
            pltpu.VMEM((own_count, width), f32),
            pltpu.VMEM(own.shape, bf16),
            pltpu.VMEM(edge_out.shape, bf16),
            pltpu.VMEM(node_in.shape, bf16),
            pltpu.VMEM(node_out.shape, bf16),
            pltpu.VMEM((1, width), f32),
            pltpu.VMEM((1, width), f32),
            pltpu.VMEM((2 * middle.shape[0], width), bf16),
            pltpu.VMEM((own_count, width), f32),
            pltpu.VMEM((own_count, width), f32),
            pltpu.VMEM(edges.shape, bf16),
            pltpu.VMEM(edges.shape, bf16),
            pltpu.SMEM((AHEAD * PAIR * blk,), jnp.int32),
            pltpu.SMEM((UNITS * blk,), jnp.int32),
            pltpu.SMEM((UNITS * blk,), jnp.int32),
            dma((6,)),
            dma((2,)),
            dma((chunks,)),
            dma((chunks,)),
            dma((chunks,)),
            dma((rows_x,)),
        ],
        out_shape=[
            jax.ShapeDtypeStruct(edges.shape, bf16),
            jax.ShapeDtypeStruct(own.shape, bf16),
            jax.ShapeDtypeStruct(middle.shape, bf16),
            jax.ShapeDtypeStruct(coarse_own.shape, bf16),
        ],
        compiler_params=pltpu.CompilerParams(vmem_limit_bytes=VMEM),
        name="edge_node_layer",
    )(block_target, live.reshape(1), *small, *large)


def body(
    fine_nodes,
    edge_states,
    middle_nodes,
    coarse_nodes,
    edge_sources,
    target_blocks,
    target_nodes,
    live_blocks,
    fine_parent,
    fine_weight,
    middle_parent,
    middle_weight,
    edge_in,
    edge_bias,
    edge_out,
    edge_bias_two,
    edge_gain,
    node_in,
    node_bias,
    node_out,
    node_bias_two,
    node_gain,
    coarse_in,
    coarse_bias,
    coarse_out,
    coarse_bias_two,
    coarse_gain,
):
    rows_x, rows_y, block_size, latent = fine_nodes.shape
    own_count = rows_x * rows_y * block_size
    edge_params = (edge_out, edge_bias_two, edge_gain)
    node_params = (node_in, node_bias, node_out, node_bias_two, node_gain)
    parents_local = fine_parent.reshape(own_count)
    weights_local = fine_weight.reshape(own_count)
    middle_rows = middle_nodes[0, 0]
    mid_parents = middle_parent[0, 0]
    mid_weights = middle_weight[0, 0]
    coarse_own = coarse_nodes.shape[0]
    devices = lax.axis_size(("gx", "gy"))
    edges = edge_states.reshape(-1, latent)
    everyone, coarse_own_rows, middle_mid, pre, table, index = exchange(
        fine_nodes,
        middle_rows,
        parents_local,
        weights_local,
        mid_parents,
        mid_weights,
        coarse_nodes,
        (coarse_in, coarse_bias, coarse_out, coarse_bias_two, coarse_gain),
        edges,
        (edge_in, edge_bias),
        target_blocks[0, 0],
        target_nodes[0, 0],
        edge_sources[0, 0],
    )
    everyone = everyone.reshape(devices * coarse_own, latent)
    nodes = (parents_local, weights_local, middle_mid, mid_parents, mid_weights, everyone, coarse_own_rows)
    edge_result, fine_result, middle_result, coarse_result = run_edges(
        fine_nodes,
        table,
        pre,
        edges,
        index,
        target_blocks[0, 0],
        target_nodes[0, 0],
        live_blocks[0, 0],
        edge_params,
        nodes,
        node_params,
    )
    return (
        fine_result.reshape(fine_nodes.shape),
        edge_result.reshape(edge_states.shape),
        middle_result.reshape(middle_nodes.shape),
        coarse_result,
    )


def solution(mesh):
    placed = (
        P("gx", "gy", None, None),
        P("gx", "gy", None, None, None),
        P("gx", "gy", None, None),
        P(("gx", "gy"), None),
        P("gx", "gy", None, None),
        P("gx", "gy", None),
        P("gx", "gy", None, None),
        P("gx", "gy"),
        P("gx", "gy", None),
        P("gx", "gy", None),
        P("gx", "gy", None),
        P("gx", "gy", None),
        P(),
        P(),
        P(),
        P(),
        P(),
        P(),
        P(),
        P(),
        P(),
        P(),
        P(),
        P(),
        P(),
        P(),
        P(),
    )
    return jax.shard_map(
        body,
        mesh=mesh,
        in_specs=placed,
        out_specs=(
            P("gx", "gy", None, None),
            P("gx", "gy", None, None, None),
            P("gx", "gy", None, None),
            P(("gx", "gy"), None),
        ),
        check_vma=False,
    )
```

```python
import functools

import jax
import jax.numpy as jnp
from jax import lax
from jax.experimental import pallas as pl
from jax.experimental.pallas import tpu as pltpu
from jax.sharding import PartitionSpec as P

epsilon = 1e-05
f32 = jnp.float32
bf16 = jnp.bfloat16
GROUP = 4
UNITS = 8
PAIR = 2
AHEAD = 2
SLOTS = 4
LANES = 128
VMEM = 64 * 1024 * 1024


def layer_norm(values, gain_vec):
    centred = values - jnp.mean(values, axis=-1, keepdims=True)
    spread = jnp.mean(centred * centred, axis=-1, keepdims=True)
    return centred * lax.rsqrt(spread + epsilon) * gain_vec


def first_dims(left, right):
    return lax.dot_general(left, right, (((0,), (0,)), ((), ())), preferred_element_type=f32)


def split_two(values):
    high = values.astype(bf16)
    return high, (values - high.astype(f32)).astype(bf16)


def activate(half):
    return half + half * jnp.tanh(half)


def centred_rows(weights):
    wide = weights.astype(f32)
    return (wide - jnp.mean(wide, axis=-1, keepdims=True)).astype(bf16)


def norm_centred(centred, gain_vec):
    spread = jnp.mean(centred * centred, axis=-1, keepdims=True)
    return centred * lax.rsqrt(spread + epsilon) * gain_vec


def exchange_kernel(
    grid_shape,
    own_hbm,
    mid_ref,
    parent_ref,
    weight_ref,
    mid_parent_ref,
    mid_weight_ref,
    coarse_ref,
    win_hbm,
    bias_ref,
    wout_hbm,
    bias_two_ref,
    gain_ref,
    edges_hbm,
    edge_in_hbm,
    tb_ref,
    tgt_ref,
    src_ref,
    edge_bias_ref,
    everyone_ref,
    result_ref,
    middle_ref,
    pre_hbm,
    table_hbm,
    index_ref,
    partial,
    arrived_x,
    summed_x,
    arrived_y,
    own_v,
    win_v,
    wout_v,
    first_w,
    target_w,
    edges_v,
    pre_v,
    target_table,
    window_ref,
    source_w,
    table,
    load_sem,
    table_store,
    edge_load,
    pre_store,
    side_send,
    side_recv,
    edge_send,
    edge_recv,
    corner_send,
    corner_recv,
    sx_send,
    sx_recv,
    sy_send,
    sy_recv,
    gx_send,
    gx_recv,
    gy_send,
    gy_recv,
):
    count_x, count_y = grid_shape
    rows_x, rows_y, blk, width = own_hbm.shape
    mids = mid_ref.shape[0]
    parts = width // LANES
    chunks = edge_load.shape[0]
    chunk_rows = edges_v.shape[0] // chunks
    at_x, at_y = lax.axis_index("gx"), lax.axis_index("gy")
    peers_x = [lax.rem(at_x + offset, count_x) for offset in range(1, count_x)]
    peers_y = [lax.rem(at_y + offset, count_y) for offset in range(1, count_y)]
    mesh_ids = pl.DeviceIdType.MESH

    barrier = pltpu.get_barrier_semaphore()
    for x in peers_x:
        pl.semaphore_signal(barrier, inc=1, device_id=(x, at_y), device_id_type=mesh_ids)
    for y in peers_y:
        pl.semaphore_signal(barrier, inc=1, device_id=(at_x, y), device_id_type=mesh_ids)

    loads = [
        pltpu.make_async_copy(own_hbm, own_v, load_sem.at[0]),
        pltpu.make_async_copy(edge_in_hbm.at[2], target_w, load_sem.at[1]),
        pltpu.make_async_copy(edge_in_hbm.at[0], first_w, load_sem.at[2]),
        pltpu.make_async_copy(edge_in_hbm.at[1], source_w, load_sem.at[3]),
        pltpu.make_async_copy(win_hbm, win_v, load_sem.at[4]),
        pltpu.make_async_copy(wout_hbm, wout_v, load_sem.at[5]),
    ]

    def edge_chunk(i):
        rows = pl.ds(i * chunk_rows, chunk_rows)
        return pltpu.make_async_copy(edges_hbm.at[rows], edges_v.at[rows], edge_load.at[i])

    def pre_chunk(i):
        rows = pl.ds(i * chunk_rows, chunk_rows)
        return pltpu.make_async_copy(pre_v.at[rows], pre_hbm.at[rows], pre_store.at[i])

    for load in loads[:3]:
        load.start()
    blocks = src_ref.shape[0]
    index_ref[pl.ds(0, blocks), :] = src_ref[...] * (width // LANES)
    extra = index_ref.shape[0] - blocks
    index_ref[pl.ds(blocks, extra), :] = jnp.zeros((extra, blk), jnp.int32)
    pl.semaphore_wait(barrier, count_x + count_y - 2)

    def remote(src, dst, send, recv, x, y):
        return pltpu.make_async_remote_copy(
            src_ref=src,
            dst_ref=dst,
            send_sem=send,
            recv_sem=recv,
            device_id=(x, y),
            device_id_type=mesh_ids,
        )

    def has_x(x):
        return (x >= 0) & (x < count_x)

    def has_y(y):
        return (y >= 0) & (y < count_y)

    pieces = [(0, 1), (rows_x - 1, 1)] + ([(1, rows_x - 2)] if rows_x > 2 else [])
    ways = [1, -1]

    def side_copy(way, piece, y):
        first, length = pieces[piece]
        column = rows_y - 1 if ways[way] == 1 else 0
        to = 0 if ways[way] == 1 else rows_y + 1
        return remote(
            own_hbm.at[pl.ds(first, length), pl.ds(column, 1)],
            window_ref.at[pl.ds(first + 1, length), pl.ds(to, 1)],
            side_send.at[way, piece],
            side_recv.at[way, piece],
            at_x,
            y,
        )

    def edge_copy(way, x):
        row = rows_x - 1 if ways[way] == 1 else 0
        to = 0 if ways[way] == 1 else rows_x + 1
        return remote(
            own_hbm.at[row], window_ref.at[to, pl.ds(1, rows_y)], edge_send.at[way], edge_recv.at[way], x, at_y
        )

    def corner_copy(way, side, x):
        row = rows_x if ways[way] == 1 else 1
        to = 0 if ways[way] == 1 else rows_x + 1
        column = 0 if ways[side] == 1 else rows_y + 1
        return remote(
            window_ref.at[row, column],
            window_ref.at[to, column],
            corner_send.at[way, side],
            corner_recv.at[way, side],
            x,
            at_y,
        )

    def start_sides(piece):
        for way in range(2):

            @pl.when(has_y(at_y + ways[way]))
            def _():
                side_copy(way, piece, at_y + ways[way]).start()

    def sum_x_copy(slot_from, slot_to, x):
        return remote(
            partial.at[slot_from], arrived_x.at[slot_to], sx_send.at[slot_from], sx_recv.at[slot_to], x, at_y
        )

    def sum_y_copy(slot_from, slot_to, y):
        return remote(
            summed_x.at[slot_from], arrived_y.at[slot_to], sy_send.at[slot_from], sy_recv.at[slot_to], at_x, y
        )

    def full_y_copy(slot, y):
        here = everyone_ref.at[at_x, slot]
        return remote(here, here, gy_send.at[y], gy_recv.at[slot], at_x, y)

    def full_x_copy(slot, x):
        here = everyone_ref.at[slot]
        return remote(here, here, gx_send.at[x], gx_recv.at[slot], x, at_y)

    start_sides(0)
    start_sides(1)
    loads[0].wait()
    for i in range(chunks):
        edge_chunk(i).start()
    for load in loads[3:]:
        load.start()
    own = own_v[...].reshape(rows_x * rows_y * blk, width)
    ids = lax.broadcasted_iota(jnp.int32, (mids, own.shape[0]), 0)
    high, low = split_two(jnp.where(ids == parent_ref[...], weight_ref[...], 0.0))
    middle = mid_ref[...].astype(f32) + jnp.dot(high, own, preferred_element_type=f32)
    middle = (middle + jnp.dot(low, own, preferred_element_type=f32)).astype(bf16)
    ids = lax.broadcasted_iota(jnp.int32, (count_x * count_y * coarse_ref.shape[0], mids), 0)
    high, low = split_two(jnp.where(ids == mid_parent_ref[...], mid_weight_ref[...], 0.0))
    sums = jnp.dot(high, middle, preferred_element_type=f32)
    sums = sums + jnp.dot(low, middle, preferred_element_type=f32)
    partial[...] = sums.reshape(partial.shape).astype(bf16)
    middle_ref[...] = middle

    for x in peers_x:
        sum_x_copy(x, at_x, x).start()

    loads[1].wait()
    made = jnp.dot(own, target_w[...], preferred_element_type=f32) * 0.5
    target_table[...] = made.astype(bf16).reshape(target_table.shape)
    loads[2].wait()
    first_w[...] = first_w[...] * 0.5

    per_row = (rows_y + 2) * blk * parts

    def fill(places, block_rows):
        made = jnp.dot(block_rows, source_w[...], preferred_element_type=f32)
        made = (made + edge_bias_ref[...]) * 0.5
        for k, (a, b) in enumerate(places):
            number = a * (rows_y + 2) + b
            for c in range(parts):
                at = pl.ds(number * blk * parts + c, blk, stride=parts)
                table[at, :] = made[k * blk : (k + 1) * blk, c * LANES : (c + 1) * LANES]

    def table_copy(a):
        at = pl.ds(a * per_row, per_row)
        return pltpu.make_async_copy(table.at[at], table_hbm.at[at], table_store.at[a])

    rows = GROUP * blk

    def group(g, carry):
        at = pl.ds(pl.multiple_of(g * rows, rows), rows)
        from_target = []
        for k in range(GROUP):
            number = g * GROUP + k
            target = tgt_ref[pl.ds(number, 1), :]
            pick = (lax.broadcasted_iota(jnp.int32, (blk, blk), 0) == target).astype(f32).astype(bf16)
            from_target.append(first_dims(pick, target_table[tb_ref[number]]))
        made = jnp.dot(edges_v[at, :], first_w[...], preferred_element_type=f32)
        pre_v[at, :] = (made + jnp.concatenate(from_target, axis=0)).astype(bf16)
        return carry

    def work(first, last):
        for i in range(first, last):
            edge_chunk(i).wait()
        lax.fori_loop(first * (chunk_rows // rows), last * (chunk_rows // rows), group, 0)
        for i in range(first, last):
            pre_chunk(i).start()

    marks = [(chunks * part) // 8 for part in range(9)]

    work(marks[0], marks[3])

    total = partial[at_x].astype(f32)
    for x in peers_x:
        sum_x_copy(x, x, x).wait_recv()
        total = total + arrived_x[x].astype(f32)
    summed_x[...] = total
    for y in peers_y:
        sum_y_copy(y, at_y, y).start()
    for way in range(2):

        @pl.when(has_x(at_x + ways[way]))
        def _():
            edge_copy(way, at_x + ways[way]).start()

    work(marks[3], marks[5])

    for side in range(2):
        from_y = at_y - ways[side]

        @pl.when(has_y(from_y))
        def _():
            side_copy(side, 0, from_y).wait_recv()
            side_copy(side, 1, from_y).wait_recv()
            for way in range(2):

                @pl.when(has_x(at_x + ways[way]))
                def _():
                    corner_copy(way, side, at_x + ways[way]).start()

    restricted = summed_x[at_y]
    for y in peers_y:
        sum_y_copy(y, y, y).wait_recv()
        restricted = restricted + arrived_y[y]
    if len(pieces) > 2:
        start_sides(2)

    loads[4].wait()
    loads[5].wait()
    coarse = coarse_ref[...]
    pre = jnp.dot(coarse, win_v[0], preferred_element_type=f32)
    pre = pre + jnp.dot(restricted.astype(bf16), win_v[1], preferred_element_type=f32)
    hidden = activate((pre + bias_ref[...]) * 0.5).astype(bf16)
    output = jnp.dot(hidden, wout_v[...], preferred_element_type=f32) + bias_two_ref[...]
    result = (coarse.astype(f32) + layer_norm(output, gain_ref[...])).astype(bf16)
    everyone_ref[at_x, at_y] = result
    result_ref[...] = result
    for y in peers_y:
        full_y_copy(at_y, y).start()

    work(marks[5], marks[7])

    for y in peers_y:
        full_y_copy(y, y).wait_recv()
    for x in peers_x:
        full_x_copy(at_x, x).start()

    work(marks[7], marks[8])

    loads[3].wait()
    fill([(a, b) for a in range(1, rows_x + 1) for b in range(1, rows_y + 1)], own)

    for way in range(2):

        @pl.when(has_x(at_x - ways[way]))
        def _():
            edge_copy(way, at_x - ways[way]).wait_recv()

        @pl.when(has_x(at_x + ways[way]))
        def _():
            edge_copy(way, at_x + ways[way]).wait_send()

        @pl.when(has_y(at_y + ways[way]))
        def _():
            for piece in range(len(pieces)):
                side_copy(way, piece, at_y + ways[way]).wait_send()

        if len(pieces) > 2:

            @pl.when(has_y(at_y - ways[way]))
            def _():
                side_copy(way, 2, at_y - ways[way]).wait_recv()

        for side in range(2):

            @pl.when(has_y(at_y - ways[side]) & has_x(at_x + ways[way]))
            def _():
                corner_copy(way, side, at_x + ways[way]).wait_send()

            @pl.when(has_y(at_y - ways[side]) & has_x(at_x - ways[way]))
            def _():
                corner_copy(way, side, at_x - ways[way]).wait_recv()

    for b in (0, rows_y + 1):
        fill([(a, b) for a in range(1, rows_x + 1)], window_ref[1 : rows_x + 1, b].reshape(rows_x * blk, width))
    for a in range(1, rows_x + 1):
        table_copy(a).start()
    for a in (0, rows_x + 1):
        fill([(a, b) for b in range(rows_y + 2)], window_ref[a].reshape((rows_y + 2) * blk, width))
        table_copy(a).start()

    for x in peers_x:
        sum_x_copy(x, at_x, x).wait_send()
        full_x_copy(at_x, x).wait_send()
        full_x_copy(x, x).wait_recv()
    for y in peers_y:
        sum_y_copy(y, at_y, y).wait_send()
        full_y_copy(at_y, y).wait_send()
    for i in range(chunks):
        pre_chunk(i).wait()
    for a in range(rows_x + 2):
        table_copy(a).wait()


def exchange(own, middle, parents, weights, mid_parents, mid_weights, coarse, params, edges, edge_params, tb, tgt, src):
    rows_x, rows_y, blk, width = own.shape
    count_x, count_y = lax.axis_size("gx"), lax.axis_size("gy")
    coarse_own = coarse.shape[0]
    coarse_in, bias, coarse_out, bias_two, gain = params
    edge_in, edge_bias = edge_params
    table_shape = ((rows_x + 2) * (rows_y + 2) * blk * (width // LANES), LANES)
    row = lambda array: array.reshape(1, -1)
    vmem = pl.BlockSpec(memory_space=pltpu.VMEM)
    smem = pl.BlockSpec(memory_space=pltpu.SMEM)
    hbm = pl.BlockSpec(memory_space=pl.ANY)
    dma = pltpu.SemaphoreType.DMA
    chunks = src.shape[0] // UNITS
    return pl.pallas_call(
        functools.partial(exchange_kernel, (count_x, count_y)),
        in_specs=[hbm] + [vmem] * 6 + [hbm, vmem, hbm, vmem, vmem, hbm, hbm, smem, vmem, vmem, vmem],
        out_specs=[vmem, vmem, vmem, hbm, hbm, vmem],
        out_shape=[
            jax.ShapeDtypeStruct((count_x, count_y, coarse_own, width), bf16),
            jax.ShapeDtypeStruct((coarse_own, width), bf16),
            jax.ShapeDtypeStruct(middle.shape, bf16),
            jax.ShapeDtypeStruct(edges.shape, bf16),
            jax.ShapeDtypeStruct(table_shape, f32),
            jax.ShapeDtypeStruct((src.shape[0] + UNITS, blk), jnp.int32),
        ],
        scratch_shapes=[
            pltpu.VMEM((count_x, count_y, coarse_own, width), bf16),
            pltpu.VMEM((count_x, count_y, coarse_own, width), bf16),
            pltpu.VMEM((count_y, coarse_own, width), f32),
            pltpu.VMEM((count_y, coarse_own, width), f32),
            pltpu.VMEM(own.shape, bf16),
            pltpu.VMEM(coarse_in.shape, bf16),
            pltpu.VMEM(coarse_out.shape, bf16),
            pltpu.VMEM(edge_in.shape[1:], bf16),
            pltpu.VMEM(edge_in.shape[1:], bf16),
            pltpu.VMEM(edges.shape, bf16),
            pltpu.VMEM(edges.shape, bf16),
            pltpu.VMEM((rows_x * rows_y, blk, width), bf16),
            pltpu.VMEM((rows_x + 2, rows_y + 2, blk, width), bf16),
            pltpu.VMEM(edge_in.shape[1:], bf16),
            pltpu.VMEM(table_shape, f32),
            dma((6,)),
            dma((rows_x + 2,)),
            dma((chunks,)),
            dma((chunks,)),
            dma((2, 3)),
            dma((2, 3)),
            dma((2,)),
            dma((2,)),
            dma((2, 2)),
            dma((2, 2)),
            dma((count_x,)),
            dma((count_x,)),
            dma((count_y,)),
            dma((count_y,)),
            dma((count_x,)),
            dma((count_x,)),
            dma((count_y,)),
            dma((count_y,)),
        ],
        compiler_params=pltpu.CompilerParams(
            collective_id=0, has_side_effects=True, vmem_limit_bytes=VMEM
        ),
        name="exchange",
    )(
        own,
        middle,
        row(parents),
        row(weights),
        row(mid_parents),
        row(mid_weights),
        coarse,
        coarse_in,
        row(bias),
        coarse_out,
        row(bias_two),
        row(gain),
        edges,
        edge_in,
        tb,
        tgt,
        src,
        row(edge_bias),
    )


def edge_kernel(
    shape,
    tb_ref,
    live_ref,
    tgt_ref,
    bias_two_ref,
    gain_ref,
    parent_ref,
    weight_ref,
    mid_ref,
    mid_parent_ref,
    mid_weight_ref,
    coarse_ref,
    coarse_own_ref,
    node_bias_ref,
    node_bias_two_ref,
    node_gain_ref,
    own_hbm,
    table_hbm,
    wout_hbm,
    node_in_hbm,
    node_out_hbm,
    index_hbm,
    pre_hbm,
    edges_hbm,
    out_hbm,
    fine_hbm,
    mid_out_ref,
    coarse_out_ref,
    table,
    bufs,
    made_out,
    total,
    own_v,
    wout_v,
    node_in_v,
    node_out_v,
    bias_two_c,
    node_bias_two_c,
    doubled,
    node_pre,
    fine_base,
    pre_v,
    edges_v,
    index_first,
    index_even,
    index_odd,
    load_sem,
    index_sem,
    pre_sem,
    edge_sem,
    out_sem,
    fine_sem,
):
    rows_x, rows_y, blk, width = shape
    parts = width // LANES
    chunks = pre_sem.shape[0]
    chunk_rows = UNITS * blk
    rows = PAIR * blk
    per_chunk = UNITS // PAIR
    units = chunks * per_chunk
    live = live_ref[0]
    mids = mid_ref.shape[0]
    copy = pltpu.make_async_copy

    loads = [
        copy(table_hbm, table, load_sem.at[1]),
        copy(wout_hbm, wout_v, load_sem.at[0]),
        copy(index_hbm.at[pl.ds(0, AHEAD * rows)], index_first, load_sem.at[2]),
        copy(own_hbm, own_v, load_sem.at[3]),
        copy(node_in_hbm, node_in_v, load_sem.at[4]),
        copy(node_out_hbm, node_out_v, load_sem.at[5]),
    ]

    def chunk_at(c):
        return pl.ds(pl.multiple_of(c * chunk_rows, chunk_rows), chunk_rows)

    def pre_load(c):
        return copy(pre_hbm.at[chunk_at(c)], pre_v.at[chunk_at(c)], pre_sem.at[c])

    def edge_load(c):
        return copy(edges_hbm.at[chunk_at(c)], edges_v.at[chunk_at(c)], edge_sem.at[c])

    def out_store(c):
        return copy(edges_v.at[chunk_at(c)], out_hbm.at[chunk_at(c)], out_sem.at[c])

    def index_load(c, half):
        at = pl.ds(pl.multiple_of(c * chunk_rows + AHEAD * rows, rows), chunk_rows)
        return copy(index_hbm.at[at], (index_even, index_odd)[half], index_sem.at[half])

    def gather(index, first, slot):
        for e in range(rows):
            at = (e // 8) * (8 * parts) + e % 8
            row = pl.multiple_of(index[first + e], parts)
            bufs[slot, pl.ds(at, parts, stride=8), :] = table[pl.ds(row, parts), :]

    def second(number, slot, side):
        found = bufs[slot].reshape(rows // 8, parts, 8, LANES)
        found = jnp.concatenate([found[:, c].reshape(rows, LANES) for c in range(parts)], axis=1)
        at = pl.ds(pl.multiple_of(number * rows, rows), rows)
        hidden = activate((pre_v[at, :].astype(f32) + found).astype(bf16))
        made_out[side] = jnp.dot(hidden, wout_v[...], preferred_element_type=f32) + bias_two_c[...]

    def finish(number, side):
        for k in range(PAIR):
            block = number * PAIR + k
            centred = made_out[side, pl.ds(k * blk, blk), :]
            alive = (block < live).astype(f32)
            spread = jnp.mean(centred * centred, axis=-1, keepdims=True)
            message = (centred * (lax.rsqrt(spread + epsilon) * alive) * gain_ref[...]).astype(bf16)
            at = pl.ds(pl.multiple_of(block * blk, blk), blk)
            edges_v[at, :] = edges_v[at, :] + message
            target = tgt_ref[pl.ds(block, 1), :]
            pick = (lax.broadcasted_iota(jnp.int32, (blk, blk), 0) == target).astype(f32).astype(bf16)
            here = pl.multiple_of(tb_ref[block] * blk, blk)
            total[pl.ds(here, blk), :] += jnp.dot(pick, message, preferred_element_type=f32)

    loads[3].start()
    loads[4].start()
    for load in loads[:3]:
        load.start()
    for half in range(2):
        index_load(half, half).start()
    for c in range(2):
        pre_load(c).start()
        edge_load(c).start()
    loads[5].start()
    total[...] = jnp.zeros_like(total)
    coarse_out_ref[...] = coarse_own_ref[...]
    bias_two = bias_two_ref[...]
    bias_two_c[...] = bias_two - jnp.mean(bias_two, axis=-1, keepdims=True)
    bias_two = node_bias_two_ref[...]
    node_bias_two_c[...] = bias_two - jnp.mean(bias_two, axis=-1, keepdims=True)

    coarse = coarse_ref[...]
    ids = lax.broadcasted_iota(jnp.int32, (coarse.shape[0], mids), 0)
    high, low = split_two(jnp.where(ids == mid_parent_ref[...], mid_weight_ref[...], 0.0))
    value = mid_ref[...].astype(f32) + first_dims(high, coarse) + first_dims(low, coarse)
    value = value.astype(bf16)
    mid_out_ref[...] = value
    doubled[pl.ds(0, mids), :] = value
    doubled[pl.ds(mids, mids), :] = value

    loads[3].wait()
    loads[4].wait()
    wide = rows_y * blk
    for a in range(rows_x):
        at = pl.ds(a * wide, wide)
        own = own_v[a].reshape(wide, width)
        node_pre[at, :] = jnp.dot(own, node_in_v[0], preferred_element_type=f32) + node_bias_ref[...]
        ids = lax.broadcasted_iota(jnp.int32, (mids, wide), 0)
        high, low = split_two(jnp.where(ids == parent_ref[:, at], weight_ref[:, at], 0.0))
        from_middle = first_dims(jnp.concatenate([high, low], axis=0), doubled[...])
        fine_base[at, :] = own.astype(f32) + from_middle
    loads[1].wait()
    wout_v[...] = centred_rows(wout_v[...])
    loads[0].wait()
    loads[2].wait()
    for u in range(AHEAD):
        gather(index_first, u * rows, u % SLOTS)
    pre_load(0).wait()
    second(0, 0, 0)

    def half_step(c, half):
        edge_load(c).wait()
        index_load(c, half).wait()

        @pl.when(c + 2 < chunks)
        def _():
            pre_load(c + 2).start()
            edge_load(c + 2).start()

        @pl.when(c + 1 < chunks)
        def _():
            pre_load(c + 1).wait()

        @pl.when(c * UNITS < live)
        def _():
            for u in range(per_chunk):
                number = c * per_chunk + u
                gather((index_even, index_odd)[half], u * rows, (u + AHEAD) % SLOTS)
                second(jnp.minimum(number + 1, units - 1), (u + 1) % SLOTS, (u + 1) % 2)
                finish(number, u % 2)

        out_store(c).start()

        @pl.when(c + 2 < chunks)
        def _():
            index_load(c + 2, half).start()

    def two_steps(i, carry):
        half_step(2 * i, 0)
        half_step(2 * i + 1, 1)
        return carry

    lax.fori_loop(0, chunks // 2, two_steps, 0)

    loads[5].wait()
    node_out_v[...] = centred_rows(node_out_v[...])
    for a in range(rows_x):
        at = pl.ds(a * wide, wide)
        pre = node_pre[at, :] + jnp.dot(total[at, :].astype(bf16), node_in_v[1], preferred_element_type=f32)
        hidden = activate(pre * 0.5).astype(bf16)
        centred = jnp.dot(hidden, node_out_v[...], preferred_element_type=f32) + node_bias_two_c[...]
        fine = fine_base[at, :] + norm_centred(centred, node_gain_ref[...])
        own_v[a] = fine.astype(bf16).reshape(own_v.shape[1:])
        copy(own_v.at[a], fine_hbm.at[a], fine_sem.at[a]).start()
    for a in range(rows_x):
        copy(own_v.at[a], fine_hbm.at[a], fine_sem.at[a]).wait()
    for c in range(chunks):
        out_store(c).wait()


def run_edges(own, table, pre, edges, index, block_target, node_target, live, edge_params, nodes, node_params):
    rows_x, rows_y, blk, width = own.shape
    edge_out, bias_two, gain = edge_params
    node_in, node_bias, node_out, node_bias_two, node_gain = node_params
    parents, weights, middle, mid_parents, mid_weights, coarse, coarse_own = nodes
    chunks = edges.shape[0] // (UNITS * blk)
    row = lambda array: array.reshape(1, -1)
    own_count = rows_x * rows_y * blk
    hbm = pl.BlockSpec(memory_space=pl.ANY)
    vmem = pl.BlockSpec(memory_space=pltpu.VMEM)
    smem = pl.BlockSpec(memory_space=pltpu.SMEM)
    dma = pltpu.SemaphoreType.DMA
    small = [node_target, row(bias_two), row(gain), row(parents), row(weights), middle]
    small += [row(mid_parents), row(mid_weights), coarse, coarse_own]
    small += [row(node_bias), row(node_bias_two), row(node_gain)]
    large = [own, table, edge_out, node_in, node_out, index.reshape(-1), pre, edges]
    return pl.pallas_call(
        functools.partial(edge_kernel, own.shape),
        in_specs=[smem] * 2 + [vmem] * len(small) + [hbm] * len(large),
        out_specs=[hbm, hbm, vmem, vmem],
        scratch_shapes=[
            pltpu.VMEM(table.shape, f32),
            pltpu.VMEM((SLOTS, PAIR * blk * width // LANES, LANES), f32),
            pltpu.VMEM((2, PAIR * blk, width), f32),
            pltpu.VMEM((own_count, width), f32),
            pltpu.VMEM(own.shape, bf16),
            pltpu.VMEM(edge_out.shape, bf16),
            pltpu.VMEM(node_in.shape, bf16),
            pltpu.VMEM(node_out.shape, bf16),
            pltpu.VMEM((1, width), f32),
            pltpu.VMEM((1, width), f32),
            pltpu.VMEM((2 * middle.shape[0], width), bf16),
            pltpu.VMEM((own_count, width), f32),
            pltpu.VMEM((own_count, width), f32),
            pltpu.VMEM(edges.shape, bf16),
            pltpu.VMEM(edges.shape, bf16),
            pltpu.SMEM((AHEAD * PAIR * blk,), jnp.int32),
            pltpu.SMEM((UNITS * blk,), jnp.int32),
            pltpu.SMEM((UNITS * blk,), jnp.int32),
            dma((6,)),
            dma((2,)),
            dma((chunks,)),
            dma((chunks,)),
            dma((chunks,)),
            dma((rows_x,)),
        ],
        out_shape=[
            jax.ShapeDtypeStruct(edges.shape, bf16),
            jax.ShapeDtypeStruct(own.shape, bf16),
            jax.ShapeDtypeStruct(middle.shape, bf16),
            jax.ShapeDtypeStruct(coarse_own.shape, bf16),
        ],
        compiler_params=pltpu.CompilerParams(vmem_limit_bytes=VMEM),
        name="edge_node_layer",
    )(block_target, live.reshape(1), *small, *large)


def body(
    fine_nodes,
    edge_states,
    middle_nodes,
    coarse_nodes,
    edge_sources,
    target_blocks,
    target_nodes,
    live_blocks,
    fine_parent,
    fine_weight,
    middle_parent,
    middle_weight,
    edge_in,
    edge_bias,
    edge_out,
    edge_bias_two,
    edge_gain,
    node_in,
    node_bias,
    node_out,
    node_bias_two,
    node_gain,
    coarse_in,
    coarse_bias,
    coarse_out,
    coarse_bias_two,
    coarse_gain,
):
    rows_x, rows_y, block_size, latent = fine_nodes.shape
    own_count = rows_x * rows_y * block_size
    edge_params = (edge_out, edge_bias_two, edge_gain)
    node_params = (node_in, node_bias, node_out, node_bias_two, node_gain)
    parents_local = fine_parent.reshape(own_count)
    weights_local = fine_weight.reshape(own_count)
    middle_rows = middle_nodes[0, 0]
    mid_parents = middle_parent[0, 0]
    mid_weights = middle_weight[0, 0]
    coarse_own = coarse_nodes.shape[0]
    devices = lax.axis_size(("gx", "gy"))
    edges = edge_states.reshape(-1, latent)
    everyone, coarse_own_rows, middle_mid, pre, table, index = exchange(
        fine_nodes,
        middle_rows,
        parents_local,
        weights_local,
        mid_parents,
        mid_weights,
        coarse_nodes,
        (coarse_in, coarse_bias, coarse_out, coarse_bias_two, coarse_gain),
        edges,
        (edge_in, edge_bias),
        target_blocks[0, 0],
        target_nodes[0, 0],
        edge_sources[0, 0],
    )
    everyone = everyone.reshape(devices * coarse_own, latent)
    nodes = (parents_local, weights_local, middle_mid, mid_parents, mid_weights, everyone, coarse_own_rows)
    edge_result, fine_result, middle_result, coarse_result = run_edges(
        fine_nodes,
        table,
        pre,
        edges,
        index,
        target_blocks[0, 0],
        target_nodes[0, 0],
        live_blocks[0, 0],
        edge_params,
        nodes,
        node_params,
    )
    return (
        fine_result.reshape(fine_nodes.shape),
        edge_result.reshape(edge_states.shape),
        middle_result.reshape(middle_nodes.shape),
        coarse_result,
    )


def solution(mesh):
    placed = (
        P("gx", "gy", None, None),
        P("gx", "gy", None, None, None),
        P("gx", "gy", None, None),
        P(("gx", "gy"), None),
        P("gx", "gy", None, None),
        P("gx", "gy", None),
        P("gx", "gy", None, None),
        P("gx", "gy"),
        P("gx", "gy", None),
        P("gx", "gy", None),
        P("gx", "gy", None),
        P("gx", "gy", None),
        P(),
        P(),
        P(),
        P(),
        P(),
        P(),
        P(),
        P(),
        P(),
        P(),
        P(),
        P(),
        P(),
        P(),
        P(),
    )
    return jax.shard_map(
        body,
        mesh=mesh,
        in_specs=placed,
        out_specs=(
            P("gx", "gy", None, None),
            P("gx", "gy", None, None, None),
            P("gx", "gy", None, None),
            P(("gx", "gy"), None),
        ),
        check_vma=False,
    )
```
